768 devices in a mesh: ctx: 96 (over x, z, core), dp: 8 (over y).
Axes of the slice: x: 4, y: 8, z: 12, core: 2. Of those that a mesh axis runs over, the one named last changes fastest.
Arguments:
- query: bfloat16 [8, 12288, 1024], P('dp', 'ctx')
- key: bfloat16 [8, 12288, 1024], P('dp', 'ctx')
- value: bfloat16 [8, 12288, 1024], P('dp', 'ctx'), may hold values from -5 to 5
- dout: bfloat16 [8, 12288, 1024], P('dp', 'ctx'), may hold values from -5 to 5
- glob_keys: bfloat16 [4, 64, 1024], replicated, may hold values from -5 to 5
- glob_values: bfloat16 [4, 64, 1024], replicated, may hold values from -5 to 5
- glob_ids: int32 [8, 2], P('dp'), may hold values from 0 to 3, all different within a row
- rand_blocks: int32 [8, 192, 3], replicated, may hold values from 0 to 191, as said below
Outputs:
- d_query: bfloat16 [8, 12288, 1024], P('dp', 'ctx')
- d_key: bfloat16 [8, 12288, 1024], P('dp', 'ctx')
- d_value: bfloat16 [8, 12288, 1024], P('dp', 'ctx')
- d_global: float32 [2, 4, 64, 1024], replicated
The draws below stay inside these ranges and needn't reach their ends.
Inputs may be any that keep to these rules, and one draw needn't show every extreme that they name: With P = 96 and o_r = (r + 1) * P // 4, rand_blocks[h, i, r] lies in the span of blocks 2 * q to 2 * (q + 1) - 1, where q = (i // 2 + o_r) mod P.
All inputs are finite; a program needn't handle non-finite values.
Results may differ from the reference program's by a relative error of at most 0.015.
Values may be sent and summed in bfloat16 or wider, within the bound.
A program may use at most 64 MiB of HBM per device.

```python
import math
import jax
import jax.numpy as jnp
from jax import lax

HEADS = 8
HS = 128
BLK = 64
RAND = 3
GTAB = 4
BLK_DEV = 2
HD = 1024
NBLK = 192
SEQ = 12288
BATCH = 8


def base_draw(key, salt):
    sub_key = jax.random.fold_in(key, salt)
    return jnp.clip(jax.random.normal(sub_key, (BATCH, SEQ, HD), jnp.float32), -4.0, 4.0)


def shared_keys(key):
    keys_base = base_draw(key, 11)
    return keys_base


def draw_key(key, part):
    return shared_keys(key).astype(jnp.bfloat16)


def draw_query(key, part):
    queries = base_draw(key, 12)
    return queries.astype(jnp.bfloat16)


def draw_rand_blocks(key, part):
    span_count = NBLK // BLK_DEV
    blocks = jnp.arange(NBLK, dtype=jnp.int32)
    owners = blocks // BLK_DEV
    slots = jnp.arange(RAND, dtype=jnp.int32)
    shifts = (slots + 1) * span_count // (RAND + 1)
    targets = (owners[:, None] + shifts[None, :]) % span_count
    inside = jax.random.randint(key, (HEADS, NBLK, RAND), 0, BLK_DEV)
    drawn = targets[None, :, :] * BLK_DEV + inside
    return drawn.astype(jnp.int32)


def block_scale(rng, dims, cuts, smallest, top_value):
    def one(dim, shards_of):
        draws = jax.random.uniform(jax.random.fold_in(jax.random.fold_in(rng, 6), dim), (shards_of,), jnp.float32, smallest / len(cuts), top_value / len(cuts))
        return jnp.repeat(jnp.exp(draws), dims[dim] // shards_of).reshape((-1,) + (1,) * (len(dims) - dim - 1))

    level = one(*cuts[0])
    for cut in cuts[1:]:
        level = level * one(*cut)
    return level


def distinct(own_key, rows, amount, top, lift):
    ranking = jax.random.permutation(jax.random.fold_in(own_key, 1), amount)
    boost = ranking
    for power in range(3):
        boost = boost * boost // amount
    boost = boost * lift // amount
    lots = jax.random.randint(jax.random.fold_in(own_key, 2), (rows, amount), 0, 4096) + boost
    sure = jax.random.permutation(jax.random.fold_in(own_key, 3), rows)[jnp.arange(amount) % rows]
    lots = jnp.where(jnp.arange(rows)[:, None] == sure[None, :], 1 << 14, lots)
    priority = lots * amount + jnp.arange(amount)
    return lax.top_k(priority.astype(jnp.int32), top)[1].astype(jnp.int32)


def bell_draw(rng, extent, spread, reach, cuts=(), kind=jnp.bfloat16):
    array = jax.random.normal(rng, extent, jnp.float32) * spread
    if len(cuts) > 0:
        array = block_scale(rng, extent, cuts, -0.22, 0.18) * array
    return jnp.clip(array, min=-reach, max=reach).astype(kind)


def setup_inputs(seed: int = 0) -> dict:
    splits = jax.random.split(jax.random.key(seed), 9)
    query = draw_query(jax.random.fold_in(splits[8], 71), 0)
    key = draw_key(jax.random.fold_in(splits[8], 71), 0)
    value = bell_draw(splits[2], (BATCH, SEQ, HD), 1.0, 5.0, ((0, 8), (1, 96)))
    dout = bell_draw(splits[3], (BATCH, SEQ, HD), 1.0, 5.0, ((0, 8), (1, 96)))
    glob_keys = bell_draw(splits[4], (GTAB, BLK, HD), 1.0, 5.0)
    glob_values = bell_draw(splits[5], (GTAB, BLK, HD), 1.0, 5.0)
    glob_ids = distinct(splits[6], BATCH, GTAB, 2, 0)
    rand_blocks = draw_rand_blocks(jax.random.fold_in(splits[8], 71), 0)
    return dict(query=query, key=key, value=value, dout=dout, glob_keys=glob_keys, glob_values=glob_values, glob_ids=glob_ids, rand_blocks=rand_blocks)


def rounded(values):
    return lax.optimization_barrier(values.astype(jnp.bfloat16)).astype(jnp.float32)

def attend(q_head, o_grad, k_head, v_head, gk_head, gv_head, key_index, key_valid):
    q_blocks = q_head.shape[0]
    head_size = q_head.shape[2]
    scaling = 1.0 / math.sqrt(head_size)
    local_lists = key_index.shape[1]
    keys_all = jnp.concatenate([jnp.take(k_head, key_index, axis=0), jnp.broadcast_to(gk_head[None], (q_blocks,) + gk_head.shape)], axis=1).reshape(q_blocks, -1, head_size)
    values_all = jnp.concatenate([jnp.take(v_head, key_index, axis=0), jnp.broadcast_to(gv_head[None], (q_blocks,) + gv_head.shape)], axis=1).reshape(q_blocks, -1, head_size)
    keep_mask = jnp.repeat(jnp.concatenate([key_valid, jnp.ones((q_blocks, 2), dtype=bool)], axis=1), BLK, axis=1)
    q_float = q_head.astype(jnp.float32)
    grad_float = o_grad.astype(jnp.float32)
    keys_float = keys_all.astype(jnp.float32)
    values_float = values_all.astype(jnp.float32)
    scores = jnp.einsum('nqd,nkd->nqk', q_float, keys_float) * scaling
    scores = jnp.where(keep_mask[:, None, :], scores, -1e+30)
    row_max = lax.optimization_barrier(jnp.max(scores, axis=-1, keepdims=True))
    exp_scores = jnp.exp(scores - row_max)
    weights = exp_scores / lax.optimization_barrier(jnp.sum(exp_scores, axis=-1, keepdims=True))
    weights_b = rounded(weights)
    attn_out = jnp.einsum('nqk,nkd->nqd', weights_b, values_float)
    row_dot = lax.optimization_barrier(jnp.sum(grad_float * attn_out, axis=-1, keepdims=True))
    prob_grad = jnp.einsum('nqd,nkd->nqk', grad_float, values_float)
    score_grad = rounded(weights * (prob_grad - row_dot) * scaling)
    q_grad = jnp.einsum('nqk,nkd->nqd', score_grad, keys_float)
    k_grad = jnp.einsum('nqk,nqd->nkd', score_grad, q_float).reshape(q_blocks, local_lists + 2, BLK, head_size)
    v_grad = jnp.einsum('nqk,nqd->nkd', weights_b, grad_float).reshape(q_blocks, local_lists + 2, BLK, head_size)
    flat_index = key_index.reshape(-1)
    k_local = jnp.zeros(k_head.shape, jnp.float32).at[flat_index].add(k_grad[:, :local_lists].reshape(-1, BLK, head_size))
    v_local = jnp.zeros(v_head.shape, jnp.float32).at[flat_index].add(v_grad[:, :local_lists].reshape(-1, BLK, head_size))
    return (q_grad, k_local, v_local, k_grad[:, local_lists:], v_grad[:, local_lists:])

def by_heads(row_array):
    block_total = row_array.shape[0] // BLK
    return row_array.reshape(block_total, BLK, HEADS, HS).transpose(2, 0, 1, 3)

def from_heads(head_array):
    return head_array.transpose(1, 2, 0, 3).reshape(-1, HEADS * HS)

def reference(query, key, value, dout, glob_keys, glob_values, glob_ids, rand_blocks):
    block_count = SEQ // BLK
    blocks = jnp.arange(block_count, dtype=jnp.int32)
    window = blocks[:, None] + jnp.arange(-1, 2, dtype=jnp.int32)[None, :]
    key_valid = jnp.concatenate([(window >= 0) & (window < block_count), jnp.ones((block_count, RAND), dtype=bool)], axis=1)
    table_grad = jnp.zeros((2, GTAB, BLK, HD), jnp.float32)
    q_grads = []
    k_grads = []
    v_grads = []
    for batch_row in range(BATCH):
        chosen = glob_ids[batch_row]
        gk_heads = jnp.take(glob_keys, chosen, axis=0).reshape(2, BLK, HEADS, HS).transpose(2, 0, 1, 3)
        gv_heads = jnp.take(glob_values, chosen, axis=0).reshape(2, BLK, HEADS, HS).transpose(2, 0, 1, 3)

        def per_head(pieces):
            q_head, o_grad, k_head, v_head, gk_head, gv_head, rand_head = pieces
            key_index = jnp.clip(jnp.concatenate([window, rand_head], axis=1), 0, block_count - 1).astype(jnp.int32)
            q_grad, k_local, v_local, gk_grad, gv_grad = attend(q_head, o_grad, k_head, v_head, gk_head, gv_head, key_index, key_valid)
            return (q_grad, k_local, v_local, lax.optimization_barrier(jnp.sum(gk_grad, axis=0)), lax.optimization_barrier(jnp.sum(gv_grad, axis=0)))
        results = lax.map(per_head, (by_heads(query[batch_row]), by_heads(dout[batch_row]), by_heads(key[batch_row]), by_heads(value[batch_row]), gk_heads, gv_heads, rand_blocks))
        q_grads.append(from_heads(results[0]).astype(jnp.bfloat16))
        k_grads.append(from_heads(results[1]).astype(jnp.bfloat16))
        v_grads.append(from_heads(results[2]).astype(jnp.bfloat16))
        gk_sum = results[3].transpose(1, 2, 0, 3).reshape(2, BLK, HD)
        gv_sum = results[4].transpose(1, 2, 0, 3).reshape(2, BLK, HD)
        table_grad = table_grad.at[0, chosen].add(gk_sum)
        table_grad = table_grad.at[1, chosen].add(gv_sum)
    return (jnp.stack(q_grads), jnp.stack(k_grads), jnp.stack(v_grads), table_grad)
```

```python
import functools
import math

import jax
import jax.numpy as jnp
from jax import lax
from jax.experimental import pallas as pl
from jax.experimental.pallas import tpu as pltpu
from jax.sharding import PartitionSpec as P

BLK = 64
HS = 128
NX = 4
SLOTS = 3
TABLE = 4
MESH = pl.DeviceIdType.MESH
BF16 = jnp.bfloat16
F32 = jnp.float32


def dot_nt(a, b):
    return lax.dot_general(a, b, (((1,), (1,)), ((), ())), preferred_element_type=F32)


def dot_nn(a, b):
    return lax.dot_general(a, b, (((1,), (0,)), ((), ())), preferred_element_type=F32)


def dot_tn(a, b):
    return lax.dot_general(a, b, (((0,), (0,)), ((), ())), preferred_element_type=F32)


def body(
    nz,
    ny,
    hx,
    ids_ref,
    rand_ref,
    q_in,
    k_in,
    v_in,
    o_in,
    gk_in,
    gv_in,
    dq_out,
    dk_out,
    dv_out,
    dg_out,
    kv,
    qd,
    edge,
    tab,
    gsel,
    pt,
    dst,
    dqs,
    dkv,
    dkvb,
    edge_s,
    edge_r,
    gp,
    gpb,
    g_core,
    y_send,
    y_recv,
    z_send,
    z_recv,
    y_all,
    in_loc,
    in_snd,
    in_rcv,
    tab_sem,
    e_snd,
    e_rcv,
    b_snd,
    b_rcv,
    dq_loc,
    dq_snd,
    dq_rcv,
    dkv_loc,
    dkv_snd,
    dkv_rcv,
    c_snd,
    c_rcv,
    yr_snd,
    yr_rcv,
    zr_snd,
    zr_rcv,
    zg_snd,
    zg_rcv,
    yg_snd,
    yg_rcv,
    xg_loc,
    xg_snd,
    xg_rcv,
    cg_snd,
    cg_rcv,
):
    ring = nz * 2
    ctx = lax.axis_index("ctx")
    y = lax.axis_index("dp")
    x = ctx // ring
    pos = ctx % ring
    z = pos // 2
    c = pos % 2
    wide = hx * HS
    scaling = 1.0 / math.sqrt(HS)
    own_cols = pl.multiple_of(x * wide, HS)
    up = x * ring + (pos + 1) % ring
    low = x * ring + (pos + ring - 1) % ring
    sib = x * ring + z * 2 + (1 - c)
    far = x * ring + jnp.where(c == 0, (pos + ring - 1) % ring, (pos + 1) % ring)

    def at_x(step):
        return (x + step) % NX

    def ctx_x(xs):
        return xs * ring + pos

    def ctx_z(zs):
        return x * ring + zs * 2 + c

    def remote(src, dst_ref, snd, rcv, to_ctx, to_y):
        return pltpu.make_async_remote_copy(
            src_ref=src,
            dst_ref=dst_ref,
            send_sem=snd,
            recv_sem=rcv,
            device_id={"ctx": to_ctx, "dp": to_y},
            device_id_type=MESH,
        )

    tab_copies = []
    for t, table in enumerate((gk_in, gv_in)):
        copy = pltpu.make_async_copy(table.at[:, :, pl.ds(own_cols, wide)], tab.at[t], tab_sem.at[t])
        copy.start()
        tab_copies.append(copy)

    tensors = (k_in, v_in, q_in, o_in)

    def land(h, t, xs):
        return (kv if t < 2 else qd).at[h, (t % 2) * NX + xs]

    local_in = {}
    for t in range(4):
        for h in range(hx):
            copy = pltpu.make_async_copy(
                tensors[t].at[:, :, pl.ds(pl.multiple_of(x * wide + h * HS, HS), HS)],
                land(h, t, x),
                in_loc.at[h, t],
            )
            copy.start()
            local_in[h, t] = copy

    barrier = pltpu.get_barrier_semaphore()
    partners = [(ctx_x(at_x(j)), y) for j in range(1, NX)]
    partners += [(sib, y), (far, y)]
    partners += [(ctx, (y + j) % ny) for j in range(1, ny)]
    partners += [(ctx_z((z + j) % nz), y) for j in range(1, nz)]
    for to_ctx, to_y in partners:
        pl.semaphore_signal(barrier, inc=1, device_id={"ctx": to_ctx, "dp": to_y}, device_id_type=MESH)
    pl.semaphore_wait(barrier, len(partners))

    sends = []

    def send_in(h, t, j):
        to = at_x(j)
        copy = remote(
            tensors[t].at[:, :, pl.ds(pl.multiple_of(to * wide + h * HS, HS), HS)],
            land(h, t, x),
            in_snd.at[h, t, j - 1],
            in_rcv.at[h, t, j - 1],
            ctx_x(to),
            y,
        )
        copy.start()
        sends.append(copy)

    def wait_in(h, t):
        local_in[h, t].wait()
        for j in (1, 3, 2):
            frm = at_x(NX - j)
            remote(
                land(h, t, frm), land(h, t, frm), in_snd.at[h, t, j - 1], in_rcv.at[h, t, j - 1], ctx_x(frm), y
            ).wait_recv()

    for pair in ((0, 1), (2, 3)):
        for h in range(hx):
            for t in pair:
                for j in (2, 1, 3):
                    send_in(h, t, j)

    for copy in tab_copies:
        copy.wait()
    for h in range(hx):
        for t in range(2):
            for s in range(2):
                gsel[h, t, s] = tab[t, ids_ref[0, s], :, h * HS : (h + 1) * HS]

    edge_copies = {}
    for h in range(hx):
        wait_in(h, 0)
        wait_in(h, 1)
        for way, to in ((0, up), (1, low)):
            copy = remote(
                kv.at[h, :, 1 - way], edge.at[h, way], e_snd.at[h, way], e_rcv.at[h, way], to, y
            )
            copy.start()
            edge_copies[h, way] = copy
            sends.append(copy)

    seam_low = jnp.where(pos == 0, 1, 0)
    seam_up = jnp.where(pos == ring - 1, 1, 0)

    def compute(h):
        k_main = kv[h, 0:NX].reshape(NX * 2 * BLK, HS)
        v_main = kv[h, NX : 2 * NX].reshape(NX * 2 * BLK, HS)
        k_tab = gsel[h, 0].reshape(2 * BLK, HS)
        v_tab = gsel[h, 1].reshape(2 * BLK, HS)
        lane = lax.broadcasted_iota(jnp.int32, (1, 2 * BLK), 1)
        half = lane // BLK

        def span(xq, carry):
            q = qd[h, xq].reshape(2 * BLK, HS)
            g = qd[h, NX + xq].reshape(2 * BLK, HS)
            i_low = (xq + NX - seam_low) % NX
            i_up = (xq + seam_up) % NX
            k_edge = jnp.concatenate([edge[h, 0, i_low], edge[h, 1, i_up]], axis=0)
            v_edge = jnp.concatenate([edge[h, 0, NX + i_low], edge[h, 1, NX + i_up]], axis=0)
            s_main = dot_nt(k_main, q) * scaling
            s_tab = dot_nt(k_tab, q) * scaling
            s_edge = dot_nt(k_edge, q) * scaling
            block = 2 * (xq * ring + pos)
            pieces = []
            for xs in range(NX):
                slot = (xs + NX - xq - 1) % NX
                row = jnp.minimum(slot, SLOTS - 1)
                first = rand_ref[row, x * hx + h, block] % 2
                second = rand_ref[row, x * hx + h, block + 1] % 2
                own = jnp.where(slot == SLOTS, 1, 0)
                inside = jnp.where(half == 0, first, second)
                for b in range(2):
                    hit = jnp.where(inside == b, 1, own)
                    keep = jnp.broadcast_to(hit, (BLK, 2 * BLK)) > 0
                    at = (xs * 2 + b) * BLK
                    pieces.append(jnp.where(keep, s_main[at : at + BLK], -1e30))
            pieces += [s_tab[:BLK], s_tab[BLK:]]
            ok_low = jnp.where(jnp.logical_and(xq == 0, pos == 0), 0, 1)
            ok_up = jnp.where(jnp.logical_and(xq == NX - 1, pos == ring - 1), 0, 1)
            for b, ok in ((0, ok_low), (1, ok_up)):
                hit = jnp.where(half == b, ok, 0)
                keep = jnp.broadcast_to(hit, (BLK, 2 * BLK)) > 0
                pieces.append(jnp.where(keep, s_edge[b * BLK : (b + 1) * BLK], -1e30))
            top = functools.reduce(jnp.maximum, pieces)
            top = jnp.max(top, axis=0, keepdims=True)
            exps = [jnp.exp(piece - top) for piece in pieces]
            total = jnp.sum(functools.reduce(jnp.add, exps), axis=0, keepdims=True)
            inverse = 1.0 / total
            d_main = dot_nt(v_main, g)
            d_tab = dot_nt(v_tab, g)
            d_edge = dot_nt(v_edge, g)
            d_pieces = [d_main[i * BLK : (i + 1) * BLK] for i in range(2 * NX)]
            d_pieces += [d_tab[:BLK], d_tab[BLK:], d_edge[:BLK], d_edge[BLK:]]
            probs = [e * inverse for e in exps]
            probs_b = [p.astype(BF16) for p in probs]
            dots = functools.reduce(
                jnp.add, [p.astype(F32) * d for p, d in zip(probs_b, d_pieces)]
            )
            row_dot = jnp.sum(dots, axis=0, keepdims=True)
            grads = [
                (p * (d - row_dot) * scaling).astype(BF16) for p, d in zip(probs, d_pieces)
            ]
            p_list = jnp.concatenate(probs_b[:10], axis=0)
            g_list = jnp.concatenate(grads[:10], axis=0)
            cols = pl.ds(pl.multiple_of(xq * 2 * BLK, 2 * BLK), 2 * BLK)
            pt[:, cols] = p_list
            dst[:, cols] = g_list
            g_edge = jnp.concatenate(grads[10:], axis=0)
            p_edge = jnp.concatenate(probs_b[10:], axis=0)
            dq = dot_tn(g_list[: NX * 2 * BLK], k_main)
            dq += dot_tn(g_list[NX * 2 * BLK :], k_tab)
            dq += dot_tn(g_edge, k_edge)
            dqs[h, xq] = dq.astype(BF16).reshape(2, BLK, HS)
            dk_edge = dot_nn(g_edge, q).astype(BF16)
            dv_edge = dot_nn(p_edge, g).astype(BF16)
            edge_s[h, 0, i_low] = dk_edge[:BLK]
            edge_s[h, 1, i_up] = dk_edge[BLK:]
            edge_s[h, 0, NX + i_low] = dv_edge[:BLK]
            edge_s[h, 1, NX + i_up] = dv_edge[BLK:]
            return carry

        lax.fori_loop(0, NX, span, 0)
        for t, lists in ((0, dst), (1, pt)):
            rows = qd[h, t * NX : (t + 1) * NX].reshape(NX * 2 * BLK, HS)
            grad = dot_nn(lists[...], rows)
            dkv[h, t * NX : (t + 1) * NX] = grad[: NX * 2 * BLK].reshape(NX, 2, BLK, HS)
            gp[t, :, :, h * HS : (h + 1) * HS] = grad[NX * 2 * BLK :].reshape(2, BLK, HS)

    back_copies = {}
    pending = []
    locals_out = []

    def out_cols(xs, h):
        return pl.ds(pl.multiple_of(xs * wide + h * HS, HS), HS)

    def send_out(out, src_of, h, snd, rcv, loc):
        for j in (2, 1, 3):
            to = at_x(j)
            copy = remote(
                src_of(to), out.at[:, :, out_cols(x, h)], snd(j - 1), rcv(j - 1), ctx_x(to), y
            )
            copy.start()
            sends.append(copy)
            frm = at_x(NX - j)
            pending.append(
                remote(
                    src_of(to), out.at[:, :, out_cols(frm, h)], snd(j - 1), rcv(j - 1), ctx_x(to), y
                )
            )
        copy = pltpu.make_async_copy(src_of(x), out.at[:, :, out_cols(x, h)], loc)
        copy.start()
        locals_out.append(copy)

    def after(h):
        for way, to in ((0, low), (1, up)):
            copy = remote(
                edge_s.at[h, way], edge_r.at[h, way], b_snd.at[h, way], b_rcv.at[h, way], to, y
            )
            copy.start()
            back_copies[h, way] = copy
            sends.append(copy)
        send_out(
            dq_out,
            lambda xs: dqs.at[h, xs],
            h,
            lambda j: dq_snd.at[h, j],
            lambda j: dq_rcv.at[h, j],
            dq_loc.at[h],
        )

    def finish(h):
        for way in range(2):
            back_copies[h, way].wait_recv()
        for t in range(2):
            for b in range(2):
                part = slice(t * NX, (t + 1) * NX)
                total = dkv[h, part, b] + edge_r[h, 1 - b, part].astype(F32)
                dkvb[h, part, b] = total.astype(BF16)
        for t, out in ((0, dk_out), (1, dv_out)):
            send_out(
                out,
                lambda xs, t=t: dkvb.at[h, t * NX + xs],
                h,
                lambda j, t=t: dkv_snd.at[h, t, j],
                lambda j, t=t: dkv_rcv.at[h, t, j],
                dkv_loc.at[h, t],
            )

    for h in range(hx):
        wait_in(h, 2)
        wait_in(h, 3)
        for way in range(2):
            edge_copies[h, way].wait_recv()
        compute(h)
        after(h)

    gpb[...] = gp[...].astype(BF16)
    core_copy = remote(gpb.at[1 - c], g_core, c_snd.at[0], c_rcv.at[0], sib, y)
    core_copy.start()
    sends.append(core_copy)
    for h in range(hx - 1):
        finish(h)
    core_copy.wait_recv()
    rows_y = TABLE * BLK // ny
    both = [gp[c, s] + g_core[s].astype(F32) for s in range(2)]
    per_block = BLK // rows_y
    for b in range(TABLE):
        value = jnp.where(ids_ref[0, 0] == b, both[0], 0.0) + jnp.where(ids_ref[0, 1] == b, both[1], 0.0)
        for r in range(per_block):
            y_send[b * per_block + r] = value[r * rows_y : (r + 1) * rows_y].astype(BF16)
    for j in range(1, ny):
        copy = remote(
            y_send.at[(y + j) % ny], y_recv.at[j - 1], yr_snd.at[j - 1], yr_rcv.at[j - 1], ctx, (y + j) % ny
        )
        copy.start()
        sends.append(copy)
    finish(hx - 1)
    for j in range(1, ny):
        remote(y_send.at[y], y_recv.at[j - 1], yr_snd.at[j - 1], yr_rcv.at[j - 1], ctx, y).wait_recv()
    total = y_send[y].astype(F32)
    for j in range(1, ny):
        total += y_recv[j - 1].astype(F32)
    parts = z_send.shape[0]
    rows_z = z_send.shape[1]
    every = nz // parts
    for k in range(parts):
        z_send[k] = total[k * rows_z : (k + 1) * rows_z].astype(BF16)
    is_owner = z % every == 0
    mine = z // every

    def z_reduce(k, j):
        return remote(
            z_send.at[k], z_recv.at[j - 1], zr_snd.at[j - 1], zr_rcv.at[j - 1], ctx_z((z + j) % nz), y
        )

    def z_gather(j, k):
        return remote(
            y_all.at[y, k], y_all.at[y, k], zg_snd.at[j - 1], zg_rcv.at[k], ctx_z((z + j) % nz), y
        )

    for j in range(1, nz):
        to = (z + j) % nz

        @pl.when(to % every == 0)
        def _(j=j, to=to):
            z_reduce(to // every, j).start()

    @pl.when(is_owner)
    def _():
        for j in range(1, nz):
            z_reduce(0, j).wait_recv()
        acc = z_send[mine].astype(F32)
        for j in range(1, nz):
            acc += z_recv[j - 1].astype(F32)
        y_all[y, mine] = acc.astype(BF16)
        for j in range(1, nz):
            z_gather(j, mine).start()

    for k in range(parts):

        @pl.when(z != k * every)
        def _(k=k):
            z_gather(1, k).wait_recv()

    for j in range(1, ny):
        copy = remote(
            y_all.at[y], y_all.at[y], yg_snd.at[j - 1], yg_rcv.at[j - 1], ctx, (y + j) % ny
        )
        copy.start()
        sends.append(copy)
    for j in range(1, ny):
        frm = (y + ny - j) % ny
        remote(y_all.at[frm], y_all.at[frm], yg_snd.at[j - 1], yg_rcv.at[j - 1], ctx, y).wait_recv()

    def table_out(xs, kind):
        return dg_out.at[kind, :, :, :, pl.ds(pl.multiple_of(xs * wide, HS), wide)]

    for j in (2, 1, 3):
        copy = remote(
            y_all, table_out(x, c), xg_snd.at[j - 1], xg_rcv.at[j - 1], ctx_x(at_x(j)), y
        )
        copy.start()
        sends.append(copy)
    copy = pltpu.make_async_copy(y_all, table_out(x, c), xg_loc.at[0])
    copy.start()
    locals_out.append(copy)

    def to_sibling(src, xs, j):
        copy = remote(src, table_out(xs, c), cg_snd.at[j], cg_rcv.at[j], sib, y)
        copy.start()
        sends.append(copy)
        pending.append(remote(src, table_out(xs, 1 - c), cg_snd.at[j], cg_rcv.at[j], sib, y))

    to_sibling(y_all, x, 0)
    for j in (1, 3, 2):
        frm = at_x(NX - j)
        remote(y_all, table_out(frm, c), xg_snd.at[j - 1], xg_rcv.at[j - 1], ctx_x(frm), y).wait_recv()
        to_sibling(table_out(frm, c), frm, j)

    for copy in pending:
        copy.wait_recv()
    for copy in locals_out:
        copy.wait()
    for copy in sends:
        copy.wait_send()
    for j in range(1, nz):
        to = (z + j) % nz

        @pl.when(to % every == 0)
        def _(j=j):
            z_reduce(0, j).wait_send()

        @pl.when(is_owner)
        def _(j=j):
            z_gather(j, mine).wait_send()


def on_device(nz, ny, query, key, value, dout, glob_keys, glob_values, glob_ids, rand_blocks):
    heads = rand_blocks.shape[0]
    hx = heads // NX
    hd = query.shape[2]
    wide = hx * HS
    rows_y = TABLE * BLK // ny
    parts = 4
    rows_z = rows_y // parts
    blocks = [a.reshape(2, BLK, hd) for a in (query, key, value, dout)]
    rand = jnp.transpose(rand_blocks, (2, 0, 1))
    vm = pltpu.VMEM
    dma = pltpu.SemaphoreType.DMA
    out = jax.ShapeDtypeStruct((2, BLK, hd), BF16)
    anywhere = pl.BlockSpec(memory_space=pl.ANY)
    scalars = pl.BlockSpec(memory_space=pltpu.SMEM)
    scratch = [
        vm((hx, 2 * NX, 2, BLK, HS), BF16),
        vm((hx, 2 * NX, 2, BLK, HS), BF16),
        vm((hx, 2, 2 * NX, BLK, HS), BF16),
        vm((2, TABLE, BLK, wide), BF16),
        vm((hx, 2, 2, BLK, HS), BF16),
        vm((10 * BLK, NX * 2 * BLK), BF16),
        vm((10 * BLK, NX * 2 * BLK), BF16),
        vm((hx, NX, 2, BLK, HS), BF16),
        vm((hx, 2 * NX, 2, BLK, HS), F32),
        vm((hx, 2 * NX, 2, BLK, HS), BF16),
        vm((hx, 2, 2 * NX, BLK, HS), BF16),
        vm((hx, 2, 2 * NX, BLK, HS), BF16),
        vm((2, 2, BLK, wide), F32),
        vm((2, 2, BLK, wide), BF16),
        vm((2, BLK, wide), BF16),
        vm((ny, rows_y, wide), BF16),
        vm((max(ny - 1, 1), rows_y, wide), BF16),
        vm((parts, rows_z, wide), BF16),
        vm((max(nz - 1, 1), rows_z, wide), BF16),
        vm((ny, parts, rows_z, wide), BF16),
        dma((hx, 4)),
        dma((hx, 4, 3)),
        dma((hx, 4, 3)),
        dma((2,)),
        dma((hx, 2)),
        dma((hx, 2)),
        dma((hx, 2)),
        dma((hx, 2)),
        dma((hx,)),
        dma((hx, 3)),
        dma((hx, 3)),
        dma((hx, 2)),
        dma((hx, 2, 3)),
        dma((hx, 2, 3)),
        dma((1,)),
        dma((1,)),
        dma((ny,)),
        dma((ny,)),
        dma((nz,)),
        dma((nz,)),
        dma((nz,)),
        dma((parts,)),
        dma((ny,)),
        dma((ny,)),
        dma((1,)),
        dma((3,)),
        dma((3,)),
        dma((4,)),
        dma((4,)),
    ]
    dq, dk, dv, dg = pl.pallas_call(
        functools.partial(body, nz, ny, hx),
        out_shape=(out, out, out, jax.ShapeDtypeStruct((2, ny, parts, rows_z, hd), BF16)),
        in_specs=[scalars, scalars] + [anywhere] * 6,
        out_specs=(anywhere,) * 4,
        scratch_shapes=scratch,
        compiler_params=pltpu.CompilerParams(
            collective_id=0, has_side_effects=True, vmem_limit_bytes=48 * 1024 * 1024
        ),
    )(glob_ids, rand, *blocks, glob_keys, glob_values)
    dq, dk, dv = (a.reshape(1, 2 * BLK, hd) for a in (dq, dk, dv))
    return dq, dk, dv, dg.reshape(2, TABLE, BLK, hd).astype(F32)


def solution(mesh):
    ny = mesh.shape["dp"]
    nz = mesh.shape["ctx"] // (2 * NX)
    split = P("dp", "ctx", None)
    return jax.shard_map(
        functools.partial(on_device, nz, ny),
        mesh=mesh,
        in_specs=(split, split, split, split, P(), P(), P("dp", None), P()),
        out_specs=(split, split, split, P()),
        check_vma=False,
    )
```

```python
import functools
import math

import jax
import jax.numpy as jnp
from jax import lax
from jax.experimental import pallas as pl
from jax.experimental.pallas import tpu as pltpu
from jax.sharding import PartitionSpec as P

BLK = 64
HS = 128
NX = 4
SLOTS = 3
TABLE = 4
MESH = pl.DeviceIdType.MESH
BF16 = jnp.bfloat16
F32 = jnp.float32


def dot_nt(a, b):
    return lax.dot_general(a, b, (((1,), (1,)), ((), ())), preferred_element_type=F32)


def dot_nn(a, b):
    return lax.dot_general(a, b, (((1,), (0,)), ((), ())), preferred_element_type=F32)


def dot_tn(a, b):
    return lax.dot_general(a, b, (((0,), (0,)), ((), ())), preferred_element_type=F32)


def outward(count):
    return sorted(range(1, count), key=lambda j: (-min(j, count - j), j))


def body(
    nz,
    ny,
    hx,
    ids_ref,
    rand_ref,
    q_in,
    k_in,
    v_in,
    o_in,
    gk_in,
    gv_in,
    dq_out,
    dk_out,
    dv_out,
    dg_out,
    kv,
    qd,
    edge,
    tab,
    gsel,
    pt,
    dst,
    dqs,
    dkv,
    dkvb,
    edge_s,
    edge_r,
    gp,
    gpb,
    g_core,
    ids_all,
    y_send,
    y_recv,
    z_all,
    y_all,
    in_loc,
    in_snd,
    in_rcv,
    tab_sem,
    e_snd,
    e_rcv,
    b_snd,
    b_rcv,
    dq_loc,
    dq_snd,
    dq_rcv,
    dkv_loc,
    dkv_snd,
    dkv_rcv,
    c_snd,
    c_rcv,
    id_snd,
    id_rcv,
    yr_snd,
    yr_rcv,
    z_snd,
    z_rcv,
    yg_snd,
    yg_rcv,
    xg_loc,
    xg_snd,
    xg_rcv,
    cg_snd,
    cg_rcv,
):
    ring = nz * 2
    ctx = lax.axis_index("ctx")
    y = lax.axis_index("dp")
    x = ctx // ring
    pos = ctx % ring
    z = pos // 2
    c = pos % 2
    wide = hx * HS
    scaling = 1.0 / math.sqrt(HS)
    own_cols = pl.multiple_of(x * wide, HS)
    up = x * ring + (pos + 1) % ring
    low = x * ring + (pos + ring - 1) % ring
    sib = x * ring + z * 2 + (1 - c)
    far = x * ring + jnp.where(c == 0, (pos + ring - 1) % ring, (pos + 1) % ring)

    def at_x(step):
        return (x + step) % NX

    def ctx_x(xs):
        return xs * ring + pos

    def ctx_z(zs):
        return x * ring + zs * 2 + c

    def remote(src, dst_ref, snd, rcv, to_ctx, to_y):
        return pltpu.make_async_remote_copy(
            src_ref=src,
            dst_ref=dst_ref,
            send_sem=snd,
            recv_sem=rcv,
            device_id={"ctx": to_ctx, "dp": to_y},
            device_id_type=MESH,
        )

    tab_copies = []
    for t, table in enumerate((gk_in, gv_in)):
        copy = pltpu.make_async_copy(table.at[:, :, pl.ds(own_cols, wide)], tab.at[t], tab_sem.at[t])
        copy.start()
        tab_copies.append(copy)

    tensors = (k_in, v_in, q_in, o_in)

    def land(h, t, xs):
        return (kv if t < 2 else qd).at[h, (t % 2) * NX + xs]

    local_in = {}
    for t in range(4):
        for h in range(hx):
            copy = pltpu.make_async_copy(
                tensors[t].at[:, :, pl.ds(pl.multiple_of(x * wide + h * HS, HS), HS)],
                land(h, t, x),
                in_loc.at[h, t],
            )
            copy.start()
            local_in[h, t] = copy

    barrier = pltpu.get_barrier_semaphore()
    partners = [(ctx_x(at_x(j)), y) for j in range(1, NX)]
    partners += [(sib, y), (far, y)]
    partners += [(ctx, (y + j) % ny) for j in range(1, ny)]
    partners += [(ctx_z((z + j) % nz), y) for j in range(1, nz)]
    for to_ctx, to_y in partners:
        pl.semaphore_signal(barrier, inc=1, device_id={"ctx": to_ctx, "dp": to_y}, device_id_type=MESH)
    pl.semaphore_wait(barrier, len(partners))

    sends = []

    def send_in(h, t, j):
        to = at_x(j)
        copy = remote(
            tensors[t].at[:, :, pl.ds(pl.multiple_of(to * wide + h * HS, HS), HS)],
            land(h, t, x),
            in_snd.at[h, t, j - 1],
            in_rcv.at[h, t, j - 1],
            ctx_x(to),
            y,
        )
        copy.start()
        sends.append(copy)

    def wait_in(h, t):
        local_in[h, t].wait()
        for j in (1, 3, 2):
            frm = at_x(NX - j)
            remote(
                land(h, t, frm), land(h, t, frm), in_snd.at[h, t, j - 1], in_rcv.at[h, t, j - 1], ctx_x(frm), y
            ).wait_recv()

    for pair in ((0, 1), (2, 3)):
        for h in range(hx):
            for t in pair:
                for j in (2, 1, 3):
                    send_in(h, t, j)

    for s in range(2):
        ids_all[y, s] = jnp.full((BLK // ny, HS), ids_ref[0, s], jnp.int32)
    id_waits = []
    for j in range(1, ny):
        to, frm = (y + j) % ny, (y + ny - j) % ny
        copy = remote(ids_all.at[y], ids_all.at[y], id_snd.at[j - 1], id_rcv.at[j - 1], ctx, to)
        copy.start()
        sends.append(copy)
        id_waits.append(
            remote(ids_all.at[frm], ids_all.at[frm], id_snd.at[j - 1], id_rcv.at[j - 1], ctx, frm)
        )

    for copy in tab_copies:
        copy.wait()
    for h in range(hx):
        for t in range(2):
            for s in range(2):
                gsel[h, t, s] = tab[t, ids_ref[0, s], :, h * HS : (h + 1) * HS]

    edge_copies = {}
    for h in range(hx):
        wait_in(h, 0)
        wait_in(h, 1)
        for way, to in ((0, up), (1, low)):
            copy = remote(
                kv.at[h, :, 1 - way], edge.at[h, way], e_snd.at[h, way], e_rcv.at[h, way], to, y
            )
            copy.start()
            edge_copies[h, way] = copy
            sends.append(copy)

    seam_low = jnp.where(pos == 0, 1, 0)
    seam_up = jnp.where(pos == ring - 1, 1, 0)

    def compute(h):
        k_main = kv[h, 0:NX].reshape(NX * 2 * BLK, HS)
        v_main = kv[h, NX : 2 * NX].reshape(NX * 2 * BLK, HS)
        k_tab = gsel[h, 0].reshape(2 * BLK, HS)
        v_tab = gsel[h, 1].reshape(2 * BLK, HS)
        lane = lax.broadcasted_iota(jnp.int32, (1, 2 * BLK), 1)
        half = lane // BLK

        def span(xq, carry):
            q = qd[h, xq].reshape(2 * BLK, HS)
            g = qd[h, NX + xq].reshape(2 * BLK, HS)
            i_low = (xq + NX - seam_low) % NX
            i_up = (xq + seam_up) % NX
            k_edge = jnp.concatenate([edge[h, 0, i_low], edge[h, 1, i_up]], axis=0)
            v_edge = jnp.concatenate([edge[h, 0, NX + i_low], edge[h, 1, NX + i_up]], axis=0)
            s_main = dot_nt(k_main, q) * scaling
            s_tab = dot_nt(k_tab, q) * scaling
            s_edge = dot_nt(k_edge, q) * scaling
            block = 2 * (xq * ring + pos)
            pieces = []
            for xs in range(NX):
                slot = (xs + NX - xq - 1) % NX
                row = jnp.minimum(slot, SLOTS - 1)
                first = rand_ref[row, x * hx + h, block] % 2
                second = rand_ref[row, x * hx + h, block + 1] % 2
                own = jnp.where(slot == SLOTS, 1, 0)
                inside = jnp.where(half == 0, first, second)
                for b in range(2):
                    hit = jnp.where(inside == b, 1, own)
                    keep = jnp.broadcast_to(hit, (BLK, 2 * BLK)) > 0
                    at = (xs * 2 + b) * BLK
                    pieces.append(jnp.where(keep, s_main[at : at + BLK], -1e30))
            pieces += [s_tab[:BLK], s_tab[BLK:]]
            ok_low = jnp.where(jnp.logical_and(xq == 0, pos == 0), 0, 1)
            ok_up = jnp.where(jnp.logical_and(xq == NX - 1, pos == ring - 1), 0, 1)
            for b, ok in ((0, ok_low), (1, ok_up)):
                hit = jnp.where(half == b, ok, 0)
                keep = jnp.broadcast_to(hit, (BLK, 2 * BLK)) > 0
                pieces.append(jnp.where(keep, s_edge[b * BLK : (b + 1) * BLK], -1e30))
            top = functools.reduce(jnp.maximum, pieces)
            top = jnp.max(top, axis=0, keepdims=True)
            exps = [jnp.exp(piece - top) for piece in pieces]
            total = jnp.sum(functools.reduce(jnp.add, exps), axis=0, keepdims=True)
            inverse = 1.0 / total
            d_main = dot_nt(v_main, g)
            d_tab = dot_nt(v_tab, g)
            d_edge = dot_nt(v_edge, g)
            d_pieces = [d_main[i * BLK : (i + 1) * BLK] for i in range(2 * NX)]
            d_pieces += [d_tab[:BLK], d_tab[BLK:], d_edge[:BLK], d_edge[BLK:]]
            probs = [e * inverse for e in exps]
            probs_b = [p.astype(BF16) for p in probs]
            dots = functools.reduce(
                jnp.add, [p.astype(F32) * d for p, d in zip(probs_b, d_pieces)]
            )
            row_dot = jnp.sum(dots, axis=0, keepdims=True)
            grads = [
                (p * (d - row_dot) * scaling).astype(BF16) for p, d in zip(probs, d_pieces)
            ]
            p_list = jnp.concatenate(probs_b[:10], axis=0)
            g_list = jnp.concatenate(grads[:10], axis=0)
            cols = pl.ds(pl.multiple_of(xq * 2 * BLK, 2 * BLK), 2 * BLK)
            pt[:, cols] = p_list
            dst[:, cols] = g_list
            g_edge = jnp.concatenate(grads[10:], axis=0)
            p_edge = jnp.concatenate(probs_b[10:], axis=0)
            dq = dot_tn(g_list[: NX * 2 * BLK], k_main)
            dq += dot_tn(g_list[NX * 2 * BLK :], k_tab)
            dq += dot_tn(g_edge, k_edge)
            dqs[h, xq] = dq.astype(BF16).reshape(2, BLK, HS)
            dk_edge = dot_nn(g_edge, q).astype(BF16)
            dv_edge = dot_nn(p_edge, g).astype(BF16)
            edge_s[h, 0, i_low] = dk_edge[:BLK]
            edge_s[h, 1, i_up] = dk_edge[BLK:]
            edge_s[h, 0, NX + i_low] = dv_edge[:BLK]
            edge_s[h, 1, NX + i_up] = dv_edge[BLK:]
            return carry

        lax.fori_loop(0, NX, span, 0)
        for t, lists in ((0, dst), (1, pt)):
            rows = qd[h, t * NX : (t + 1) * NX].reshape(NX * 2 * BLK, HS)
            grad = dot_nn(lists[...], rows)
            dkv[h, t * NX : (t + 1) * NX] = grad[: NX * 2 * BLK].reshape(NX, 2, BLK, HS)
            gp[t, :, :, h * HS : (h + 1) * HS] = grad[NX * 2 * BLK :].reshape(2, BLK, HS)

    back_copies = {}
    pending = []
    locals_out = []

    def out_cols(xs, h):
        return pl.ds(pl.multiple_of(xs * wide + h * HS, HS), HS)

    def send_out(out, src_of, h, snd, rcv, loc):
        for j in (2, 1, 3):
            to = at_x(j)
            copy = remote(
                src_of(to), out.at[:, :, out_cols(x, h)], snd(j - 1), rcv(j - 1), ctx_x(to), y
            )
            copy.start()
            sends.append(copy)
            frm = at_x(NX - j)
            pending.append(
                remote(
                    src_of(to), out.at[:, :, out_cols(frm, h)], snd(j - 1), rcv(j - 1), ctx_x(to), y
                )
            )
        copy = pltpu.make_async_copy(src_of(x), out.at[:, :, out_cols(x, h)], loc)
        copy.start()
        locals_out.append(copy)

    def after(h):
        for way, to in ((0, low), (1, up)):
            copy = remote(
                edge_s.at[h, way], edge_r.at[h, way], b_snd.at[h, way], b_rcv.at[h, way], to, y
            )
            copy.start()
            back_copies[h, way] = copy
            sends.append(copy)
        send_out(
            dq_out,
            lambda xs: dqs.at[h, xs],
            h,
            lambda j: dq_snd.at[h, j],
            lambda j: dq_rcv.at[h, j],
            dq_loc.at[h],
        )

    def finish(h):
        for way in range(2):
            back_copies[h, way].wait_recv()
        for t in range(2):
            for b in range(2):
                part = slice(t * NX, (t + 1) * NX)
                total = dkv[h, part, b] + edge_r[h, 1 - b, part].astype(F32)
                dkvb[h, part, b] = total.astype(BF16)
        for t, out in ((0, dk_out), (1, dv_out)):
            send_out(
                out,
                lambda xs, t=t: dkvb.at[h, t * NX + xs],
                h,
                lambda j, t=t: dkv_snd.at[h, t, j],
                lambda j, t=t: dkv_rcv.at[h, t, j],
                dkv_loc.at[h, t],
            )

    for h in range(hx):
        wait_in(h, 2)
        wait_in(h, 3)
        for way in range(2):
            edge_copies[h, way].wait_recv()
        compute(h)
        after(h)

    gpb[...] = gp[...].astype(BF16)
    core_copy = remote(gpb.at[1 - c], g_core, c_snd.at[0], c_rcv.at[0], sib, y)
    core_copy.start()
    sends.append(core_copy)
    for h in range(hx - 1):
        finish(h)
    core_copy.wait_recv()
    rows_y = BLK // ny
    for s in range(2):
        both = (gp[c, s] + g_core[s].astype(F32)).astype(BF16)
        for r in range(ny):
            y_send[r, s] = both[r * rows_y : (r + 1) * rows_y]
    for j in outward(ny):
        to = (y + j) % ny
        copy = remote(y_send.at[to], y_recv.at[y], yr_snd.at[j - 1], yr_rcv.at[j - 1], ctx, to)
        copy.start()
        sends.append(copy)
    y_recv[y] = y_send[y]
    finish(hx - 1)
    for copy in id_waits:
        copy.wait_recv()
    for j in outward(ny)[::-1]:
        frm = (y + ny - j) % ny
        remote(y_send.at[y], y_recv.at[frm], yr_snd.at[j - 1], yr_rcv.at[j - 1], ctx, frm).wait_recv()
    sums = [jnp.zeros((rows_y, wide), F32) for _ in range(TABLE)]
    for src in range(ny):
        for s in range(2):
            chosen = jnp.concatenate([ids_all[src, s]] * hx, axis=1)
            term = y_recv[src, s].astype(F32)
            sums = [acc + jnp.where(chosen == b, term, 0.0) for b, acc in enumerate(sums)]
    for b in range(TABLE):
        z_all[z, b] = sums[b].astype(BF16)
    for j in outward(nz):
        to = (z + j) % nz
        copy = remote(z_all.at[z], z_all.at[z], z_snd.at[j - 1], z_rcv.at[j - 1], ctx_z(to), y)
        copy.start()
        sends.append(copy)
    for j in outward(nz)[::-1]:
        frm = (z + nz - j) % nz
        remote(z_all.at[frm], z_all.at[frm], z_snd.at[j - 1], z_rcv.at[j - 1], ctx_z(frm), y).wait_recv()
    total = z_all[0].astype(F32)
    for k in range(1, nz):
        total += z_all[k].astype(F32)
    y_all[y] = total.astype(BF16)

    def table_out(kind, yy, xs):
        return dg_out.at[kind, :, yy, :, pl.ds(pl.multiple_of(xs * wide, HS), wide)]

    for j in outward(ny):
        to = (y + j) % ny
        copy = remote(y_all.at[y], y_all.at[y], yg_snd.at[j - 1], yg_rcv.at[j - 1], ctx, to)
        copy.start()
        sends.append(copy)

    def to_sibling(src, yy, xs, j, d):
        copy = remote(src, table_out(c, yy, xs), cg_snd.at[j, d], cg_rcv.at[j, d], sib, y)
        copy.start()
        sends.append(copy)
        pending.append(
            remote(src, table_out(1 - c, yy, xs), cg_snd.at[j, d], cg_rcv.at[j, d], sib, y)
        )

    def spread(d):
        yy = (y + ny - d) % ny
        for j in (2, 1, 3):
            copy = remote(
                y_all.at[yy],
                table_out(c, yy, x),
                xg_snd.at[j - 1, d],
                xg_rcv.at[j - 1, d],
                ctx_x(at_x(j)),
                y,
            )
            copy.start()
            sends.append(copy)
        to_sibling(y_all.at[yy], yy, x, 0, d)
        copy = pltpu.make_async_copy(y_all.at[yy], table_out(c, yy, x), xg_loc.at[d])
        copy.start()
        locals_out.append(copy)

    def pass_on(d):
        yy = (y + ny - d) % ny
        for j in (1, 3, 2):
            frm = at_x(NX - j)
            remote(
                y_all.at[yy],
                table_out(c, yy, frm),
                xg_snd.at[j - 1, d],
                xg_rcv.at[j - 1, d],
                ctx_x(frm),
                y,
            ).wait_recv()
            to_sibling(table_out(c, yy, frm), yy, frm, j, d)

    spread(0)
    before = [0]
    near = outward(ny)[::-1]
    for start in range(0, len(near), 2):
        group = near[start : start + 2]
        for d in group:
            frm = (y + ny - d) % ny
            remote(
                y_all.at[frm], y_all.at[frm], yg_snd.at[d - 1], yg_rcv.at[d - 1], ctx, frm
            ).wait_recv()
            spread(d)
        for d in before:
            pass_on(d)
        before = group
    for d in before:
        pass_on(d)

    for copy in pending:
        copy.wait_recv()
    for copy in locals_out:
        copy.wait()
    for copy in sends:
        copy.wait_send()


def last_step(dq_in, dk_in, dv_in, dg_in, dq_out, dk_out, dv_out, dg_out, narrow, full, moved, got, put):
    moves = []
    for i, (src, dst_ref) in enumerate(((dq_in, dq_out), (dk_in, dk_out), (dv_in, dv_out))):
        copy = pltpu.make_async_copy(src, dst_ref, moved.at[i])
        copy.start()
        moves.append(copy)
    parts = narrow.shape[0]
    loads = []
    for i in range(parts):
        copy = pltpu.make_async_copy(dg_in.at[i // TABLE, i % TABLE], narrow.at[i], got.at[i])
        copy.start()
        loads.append(copy)
    for i in range(parts):
        loads[i].wait()
        full[i] = narrow[i].astype(F32)
        copy = pltpu.make_async_copy(full.at[i], dg_out.at[i // TABLE, i % TABLE], put.at[i])
        copy.start()
        moves.append(copy)
    for copy in moves:
        copy.wait()


def on_device(nz, ny, query, key, value, dout, glob_keys, glob_values, glob_ids, rand_blocks):
    heads = rand_blocks.shape[0]
    hx = heads // NX
    hd = query.shape[2]
    wide = hx * HS
    rows_y = BLK // ny
    blocks = [a.reshape(2, BLK, hd) for a in (query, key, value, dout)]
    rand = jnp.transpose(rand_blocks, (2, 0, 1))
    vm = pltpu.VMEM
    dma = pltpu.SemaphoreType.DMA
    out = jax.ShapeDtypeStruct((2, BLK, hd), BF16)
    anywhere = pl.BlockSpec(memory_space=pltpu.HBM)
    scalars = pl.BlockSpec(memory_space=pltpu.SMEM)
    scratch = [
        vm((hx, 2 * NX, 2, BLK, HS), BF16),
        vm((hx, 2 * NX, 2, BLK, HS), BF16),
        vm((hx, 2, 2 * NX, BLK, HS), BF16),
        vm((2, TABLE, BLK, wide), BF16),
        vm((hx, 2, 2, BLK, HS), BF16),
        vm((10 * BLK, NX * 2 * BLK), BF16),
        vm((10 * BLK, NX * 2 * BLK), BF16),
        vm((hx, NX, 2, BLK, HS), BF16),
        vm((hx, 2 * NX, 2, BLK, HS), F32),
        vm((hx, 2 * NX, 2, BLK, HS), BF16),
        vm((hx, 2, 2 * NX, BLK, HS), BF16),
        vm((hx, 2, 2 * NX, BLK, HS), BF16),
        vm((2, 2, BLK, wide), F32),
        vm((2, 2, BLK, wide), BF16),
        vm((2, BLK, wide), BF16),
        vm((ny, 2, rows_y, HS), jnp.int32),
        vm((ny, 2, rows_y, wide), BF16),
        vm((ny, 2, rows_y, wide), BF16),
        vm((nz, TABLE, rows_y, wide), BF16),
        vm((ny, TABLE, rows_y, wide), BF16),
        dma((hx, 4)),
        dma((hx, 4, 3)),
        dma((hx, 4, 3)),
        dma((2,)),
        dma((hx, 2)),
        dma((hx, 2)),
        dma((hx, 2)),
        dma((hx, 2)),
        dma((hx,)),
        dma((hx, 3)),
        dma((hx, 3)),
        dma((hx, 2)),
        dma((hx, 2, 3)),
        dma((hx, 2, 3)),
        dma((1,)),
        dma((1,)),
        dma((ny,)),
        dma((ny,)),
        dma((ny,)),
        dma((ny,)),
        dma((nz,)),
        dma((nz,)),
        dma((ny,)),
        dma((ny,)),
        dma((ny,)),
        dma((3, ny)),
        dma((3, ny)),
        dma((4, ny)),
        dma((4, ny)),
    ]
    dq, dk, dv, dg = pl.pallas_call(
        functools.partial(body, nz, ny, hx),
        out_shape=(out, out, out, jax.ShapeDtypeStruct((2, TABLE, ny, rows_y, hd), BF16)),
        in_specs=[scalars, scalars] + [anywhere] * 6,
        out_specs=(anywhere,) * 4,
        scratch_shapes=scratch,
        compiler_params=pltpu.CompilerParams(
            collective_id=0, has_side_effects=True, vmem_limit_bytes=60 * 1024 * 1024
        ),
    )(glob_ids, rand, *blocks, glob_keys, glob_values)
    rows = jax.ShapeDtypeStruct((1, 2 * BLK, hd), BF16)
    dq, dk, dv = (a.reshape(1, 2 * BLK, hd) for a in (dq, dk, dv))
    parts = 2 * TABLE
    return tuple(
        pl.pallas_call(
            last_step,
            out_shape=(rows, rows, rows, jax.ShapeDtypeStruct((2, TABLE, BLK, hd), F32)),
            in_specs=[anywhere] * 4,
            out_specs=(anywhere,) * 4,
            scratch_shapes=[
                vm((parts, BLK, hd), BF16),
                vm((parts, BLK, hd), F32),
                dma((3,)),
                dma((parts,)),
                dma((parts,)),
            ],
            compiler_params=pltpu.CompilerParams(vmem_limit_bytes=60 * 1024 * 1024),
        )(dq, dk, dv, dg.reshape(2, TABLE, BLK, hd))
    )


def solution(mesh):
    ny = mesh.shape["dp"]
    nz = mesh.shape["ctx"] // (2 * NX)
    split = P("dp", "ctx", None)
    return jax.shard_map(
        functools.partial(on_device, nz, ny),
        mesh=mesh,
        in_specs=(split, split, split, split, P(), P(), P("dp", None), P()),
        out_specs=(split, split, split, P()),
        check_vma=False,
    )
```

```python
import functools
import math

import jax
import jax.numpy as jnp
from jax import lax
from jax.experimental import pallas as pl
from jax.experimental.pallas import tpu as pltpu
from jax.sharding import PartitionSpec as P

BLK = 64
HS = 128
NX = 4
SLOTS = 3
TABLE = 4
MESH = pl.DeviceIdType.MESH
BF16 = jnp.bfloat16
F32 = jnp.float32


def dot_nt(a, b):
    return lax.dot_general(a, b, (((1,), (1,)), ((), ())), preferred_element_type=F32)


def dot_nn(a, b):
    return lax.dot_general(a, b, (((1,), (0,)), ((), ())), preferred_element_type=F32)


def dot_tn(a, b):
    return lax.dot_general(a, b, (((0,), (0,)), ((), ())), preferred_element_type=F32)


def outward(count):
    return sorted(range(1, count), key=lambda j: (-min(j, count - j), j))


def body(
    nz,
    ny,
    hx,
    ids_ref,
    rand_ref,
    q_in,
    k_in,
    v_in,
    o_in,
    gk_in,
    gv_in,
    dq_out,
    dk_out,
    dv_out,
    dg_out,
    kv,
    qd,
    edge,
    tab,
    gsel,
    pt,
    dst,
    dqs,
    dkv,
    dkvb,
    edge_s,
    edge_r,
    gp,
    gpb,
    g_core,
    ids_all,
    y_send,
    y_recv,
    z_all,
    y_all,
    table,
    in_loc,
    in_snd,
    in_rcv,
    tab_sem,
    e_snd,
    e_rcv,
    b_snd,
    b_rcv,
    dq_loc,
    dq_snd,
    dq_rcv,
    dkv_loc,
    dkv_snd,
    dkv_rcv,
    c_snd,
    c_rcv,
    id_snd,
    id_rcv,
    yr_snd,
    yr_rcv,
    z_snd,
    z_rcv,
    yg_snd,
    yg_rcv,
    xg_loc,
    t_out,
    xg_snd,
    xg_rcv,
    cg_snd,
    cg_rcv,
    word,
):
    ring = nz * 2
    ctx = lax.axis_index("ctx")
    y = lax.axis_index("dp")
    x = ctx // ring
    pos = ctx % ring
    z = pos // 2
    c = pos % 2
    wide = hx * HS
    scaling = 1.0 / math.sqrt(HS)
    own_cols = pl.multiple_of(x * wide, HS)
    up = x * ring + (pos + 1) % ring
    low = x * ring + (pos + ring - 1) % ring
    sib = x * ring + z * 2 + (1 - c)
    far = x * ring + jnp.where(c == 0, (pos + ring - 1) % ring, (pos + 1) % ring)

    def at_x(step):
        return (x + step) % NX

    def ctx_x(xs):
        return xs * ring + pos

    def ctx_z(zs):
        return x * ring + zs * 2 + c

    def remote(src, dst_ref, snd, rcv, to_ctx, to_y):
        return pltpu.make_async_remote_copy(
            src_ref=src,
            dst_ref=dst_ref,
            send_sem=snd,
            recv_sem=rcv,
            device_id={"ctx": to_ctx, "dp": to_y},
            device_id_type=MESH,
        )

    tab_copies = []
    for t, blocks in enumerate((gk_in, gv_in)):
        copy = pltpu.make_async_copy(blocks.at[:, :, pl.ds(own_cols, wide)], tab.at[t], tab_sem.at[t])
        copy.start()
        tab_copies.append(copy)

    tensors = (k_in, v_in, q_in, o_in)

    def land(h, t, xs):
        return (kv if t < 2 else qd).at[h, (t % 2) * NX + xs]

    local_in = {}
    for t in range(4):
        for h in range(hx):
            copy = pltpu.make_async_copy(
                tensors[t].at[:, :, pl.ds(pl.multiple_of(x * wide + h * HS, HS), HS)],
                land(h, t, x),
                in_loc.at[h, t],
            )
            copy.start()
            local_in[h, t] = copy

    beside = [(ctx, (y + 1) % ny), (ctx, (y + ny - 1) % ny)]
    beside += [(ctx_z((z + 1) % nz), y), (ctx_z((z + nz - 1) % nz), y)]

    def pass_word(k):
        for i, (to_ctx, to_y) in enumerate(beside):
            if k <= (ny if i < 2 else nz) // 2 - 1:
                pl.semaphore_signal(
                    word.at[k - 1, i], inc=1, device_id={"ctx": to_ctx, "dp": to_y}, device_id_type=MESH
                )

    def hear_word(k):
        for i in range(4):
            if k <= (ny if i < 2 else nz) // 2 - 1:
                pl.semaphore_wait(word.at[k - 1, i], 1)
        pass_word(k + 1)

    barrier = pltpu.get_barrier_semaphore()
    partners = [(ctx_x(at_x(j)), y) for j in range(1, NX)]
    partners += [(sib, y), (far, y)]
    partners += beside
    for to_ctx, to_y in partners:
        pl.semaphore_signal(barrier, inc=1, device_id={"ctx": to_ctx, "dp": to_y}, device_id_type=MESH)
    pl.semaphore_wait(barrier, len(partners))
    pass_word(1)

    sends = []

    def send_in(h, t, j):
        to = at_x(j)
        copy = remote(
            tensors[t].at[:, :, pl.ds(pl.multiple_of(to * wide + h * HS, HS), HS)],
            land(h, t, x),
            in_snd.at[h, t, j - 1],
            in_rcv.at[h, t, j - 1],
            ctx_x(to),
            y,
        )
        copy.start()
        sends.append(copy)

    def wait_in(h, t):
        local_in[h, t].wait()
        for j in (1, 3, 2):
            frm = at_x(NX - j)
            remote(
                land(h, t, frm), land(h, t, frm), in_snd.at[h, t, j - 1], in_rcv.at[h, t, j - 1], ctx_x(frm), y
            ).wait_recv()

    for h in range(hx):
        for t in range(2):
            for j in (2, 1, 3):
                send_in(h, t, j)
        for j in (1, 3, 2):
            for t in range(2, 4):
                send_in(h, t, j)

    for s in range(2):
        ids_all[y, s] = jnp.full((BLK // ny, HS), ids_ref[0, s], jnp.int32)
    for copy in tab_copies:
        copy.wait()
    for h in range(hx):
        for t in range(2):
            for s in range(2):
                gsel[h, t, s] = tab[t, ids_ref[0, s], :, h * HS : (h + 1) * HS]

    edge_copies = {}


    def send_edges(h):
        wait_in(h, 0)
        wait_in(h, 1)
        for way, to in ((0, up), (1, low)):
            copy = remote(
                kv.at[h, :, 1 - way], edge.at[h, way], e_snd.at[h, way], e_rcv.at[h, way], to, y
            )
            copy.start()
            edge_copies[h, way] = copy
            sends.append(copy)

    seam_low = jnp.where(pos == 0, 1, 0)
    seam_up = jnp.where(pos == ring - 1, 1, 0)

    def compute(h):
        k_main = kv[h, 0:NX].reshape(NX * 2 * BLK, HS)
        v_main = kv[h, NX : 2 * NX].reshape(NX * 2 * BLK, HS)
        k_tab = gsel[h, 0].reshape(2 * BLK, HS)
        v_tab = gsel[h, 1].reshape(2 * BLK, HS)
        lane = lax.broadcasted_iota(jnp.int32, (1, 2 * BLK), 1)
        half = lane // BLK

        def span(i, carry):
            off = jnp.where(i == 1, NX - 1, jnp.where(i == 0, 0, i - 1))
            xq = (x + off) % NX
            sem = jnp.where(i == 1, 0, jnp.where(i == 2, 2, 1))

            @pl.when(i > 0)
            def _():
                for t in range(2, 4):
                    remote(
                        land(h, t, xq), land(h, t, xq), in_snd.at[h, t, sem], in_rcv.at[h, t, sem], ctx_x(xq), y
                    ).wait_recv()

            q = qd[h, xq].reshape(2 * BLK, HS)
            g = qd[h, NX + xq].reshape(2 * BLK, HS)
            i_low = (xq + NX - seam_low) % NX
            i_up = (xq + seam_up) % NX
            k_edge = jnp.concatenate([edge[h, 0, i_low], edge[h, 1, i_up]], axis=0)
            v_edge = jnp.concatenate([edge[h, 0, NX + i_low], edge[h, 1, NX + i_up]], axis=0)
            s_main = dot_nt(k_main, q) * scaling
            s_tab = dot_nt(k_tab, q) * scaling
            s_edge = dot_nt(k_edge, q) * scaling
            block = 2 * (xq * ring + pos)
            pieces = []
            for xs in range(NX):
                slot = (xs + NX - xq - 1) % NX
                row = jnp.minimum(slot, SLOTS - 1)
                first = rand_ref[row, x * hx + h, block] % 2
                second = rand_ref[row, x * hx + h, block + 1] % 2
                own = jnp.where(slot == SLOTS, 1, 0)
                inside = jnp.where(half == 0, first, second)
                for b in range(2):
                    hit = jnp.where(inside == b, 1, own)
                    keep = jnp.broadcast_to(hit, (BLK, 2 * BLK)) > 0
                    at = (xs * 2 + b) * BLK
                    pieces.append(jnp.where(keep, s_main[at : at + BLK], -1e30))
            pieces += [s_tab[:BLK], s_tab[BLK:]]
            ok_low = jnp.where(jnp.logical_and(xq == 0, pos == 0), 0, 1)
            ok_up = jnp.where(jnp.logical_and(xq == NX - 1, pos == ring - 1), 0, 1)
            for b, ok in ((0, ok_low), (1, ok_up)):
                hit = jnp.where(half == b, ok, 0)
                keep = jnp.broadcast_to(hit, (BLK, 2 * BLK)) > 0
                pieces.append(jnp.where(keep, s_edge[b * BLK : (b + 1) * BLK], -1e30))
            top = functools.reduce(jnp.maximum, pieces)
            top = jnp.max(top, axis=0, keepdims=True)
            exps = [jnp.exp(piece - top) for piece in pieces]
            total = jnp.sum(functools.reduce(jnp.add, exps), axis=0, keepdims=True)
            inverse = 1.0 / total
            d_main = dot_nt(v_main, g)
            d_tab = dot_nt(v_tab, g)
            d_edge = dot_nt(v_edge, g)
            d_pieces = [d_main[i * BLK : (i + 1) * BLK] for i in range(2 * NX)]
            d_pieces += [d_tab[:BLK], d_tab[BLK:], d_edge[:BLK], d_edge[BLK:]]
            probs = [e * inverse for e in exps]
            probs_b = [p.astype(BF16) for p in probs]
            dots = functools.reduce(
                jnp.add, [p.astype(F32) * d for p, d in zip(probs_b, d_pieces)]
            )
            row_dot = jnp.sum(dots, axis=0, keepdims=True)
            grads = [
                (p * (d - row_dot) * scaling).astype(BF16) for p, d in zip(probs, d_pieces)
            ]
            p_list = jnp.concatenate(probs_b[:10], axis=0)
            g_list = jnp.concatenate(grads[:10], axis=0)
            cols = pl.ds(pl.multiple_of(xq * 2 * BLK, 2 * BLK), 2 * BLK)
            pt[:, cols] = p_list
            dst[:, cols] = g_list
            g_edge = jnp.concatenate(grads[10:], axis=0)
            p_edge = jnp.concatenate(probs_b[10:], axis=0)
            dq = dot_tn(g_list[: NX * 2 * BLK], k_main)
            dq += dot_tn(g_list[NX * 2 * BLK :], k_tab)
            dq += dot_tn(g_edge, k_edge)
            dqs[h, xq] = dq.astype(BF16).reshape(2, BLK, HS)
            dk_edge = dot_nn(g_edge, q).astype(BF16)
            dv_edge = dot_nn(p_edge, g).astype(BF16)
            edge_s[h, 0, i_low] = dk_edge[:BLK]
            edge_s[h, 1, i_up] = dk_edge[BLK:]
            edge_s[h, 0, NX + i_low] = dv_edge[:BLK]
            edge_s[h, 1, NX + i_up] = dv_edge[BLK:]
            return carry

        for t in range(2, 4):
            local_in[h, t].wait()
        lax.fori_loop(0, NX, span, 0)

    last_row = NX * 2 * BLK

    def tables(h):
        for t, lists in ((0, dst), (1, pt)):
            rows = qd[h, t * NX : (t + 1) * NX].reshape(NX * 2 * BLK, HS)
            grad = dot_nn(lists[last_row:], rows).reshape(2, BLK, HS)
            gp[h, t] = grad
            gpb[h, t] = grad.astype(BF16)
        copy = remote(gpb.at[h, 1 - c], g_core.at[h], c_snd.at[h], c_rcv.at[h], sib, y)
        copy.start()
        core_copies[h] = copy
        sends.append(copy)

    def mains(h):
        for t, lists in ((0, dst), (1, pt)):
            rows = qd[h, t * NX : (t + 1) * NX].reshape(NX * 2 * BLK, HS)
            grad = dot_nn(lists[:last_row], rows)
            dkv[h, t * NX : (t + 1) * NX] = grad.reshape(NX, 2, BLK, HS)

    core_copies = {}
    back_copies = {}
    pending = []
    locals_out = []

    def out_cols(xs, h):
        return pl.ds(pl.multiple_of(xs * wide + h * HS, HS), HS)

    def send_out(out, src_of, h, snd, rcv, loc):
        for j in (2, 1, 3):
            to = at_x(j)
            copy = remote(
                src_of(to), out.at[:, :, out_cols(x, h)], snd(j - 1), rcv(j - 1), ctx_x(to), y
            )
            copy.start()
            sends.append(copy)
            frm = at_x(NX - j)
            pending.append(
                remote(
                    src_of(to), out.at[:, :, out_cols(frm, h)], snd(j - 1), rcv(j - 1), ctx_x(to), y
                )
            )
        copy = pltpu.make_async_copy(src_of(x), out.at[:, :, out_cols(x, h)], loc)
        copy.start()
        locals_out.append(copy)

    def send_back(h):
        for way, to in ((0, low), (1, up)):
            copy = remote(
                edge_s.at[h, way], edge_r.at[h, way], b_snd.at[h, way], b_rcv.at[h, way], to, y
            )
            copy.start()
            back_copies[h, way] = copy
            sends.append(copy)

    def send_dq(h):
        send_out(
            dq_out,
            lambda xs: dqs.at[h, xs],
            h,
            lambda j: dq_snd.at[h, j],
            lambda j: dq_rcv.at[h, j],
            dq_loc.at[h],
        )

    def finish(h):
        for way in range(2):
            back_copies[h, way].wait_recv()
        for t in range(2):
            for b in range(2):
                part = slice(t * NX, (t + 1) * NX)
                total = dkv[h, part, b] + edge_r[h, 1 - b, part].astype(F32)
                dkvb[h, part, b] = total.astype(BF16)
        for t, out in ((0, dk_out), (1, dv_out)):
            send_out(
                out,
                lambda xs, t=t: dkvb.at[h, t * NX + xs],
                h,
                lambda j, t=t: dkv_snd.at[h, t, j],
                lambda j, t=t: dkv_rcv.at[h, t, j],
                dkv_loc.at[h, t],
            )

    rows_y = BLK // ny

    def y_start(h):
        core_copies[h].wait_recv()
        for s in range(2):
            both = (gp[h, c, s] + g_core[h, s].astype(F32)).astype(BF16)
            for r in range(ny):
                y_send[h, r, s] = both[r * rows_y : (r + 1) * rows_y]
        for j in outward(ny):
            to = (y + j) % ny
            copy = remote(
                y_send.at[h, to], y_recv.at[h, y], yr_snd.at[h, j - 1], yr_rcv.at[h, j - 1], ctx, to
            )
            copy.start()
            sends.append(copy)
        y_recv[h, y] = y_send[h, y]

    def z_start(h):
        for j in outward(ny)[::-1]:
            frm = (y + ny - j) % ny
            remote(
                y_send.at[h, y], y_recv.at[h, frm], yr_snd.at[h, j - 1], yr_rcv.at[h, j - 1], ctx, frm
            ).wait_recv()
        sums = [jnp.zeros((rows_y, HS), F32) for _ in range(TABLE)]
        for src in range(ny):
            for s in range(2):
                chosen = ids_all[src, s]
                term = y_recv[h, src, s].astype(F32)
                sums = [acc + jnp.where(chosen == b, term, 0.0) for b, acc in enumerate(sums)]
        for b in range(TABLE):
            z_all[h, z, b] = sums[b].astype(BF16)
        for j in outward(nz):
            to = (z + j) % nz
            copy = remote(
                z_all.at[h, z], z_all.at[h, z], z_snd.at[h, j - 1], z_rcv.at[h, j - 1], ctx_z(to), y
            )
            copy.start()
            sends.append(copy)

    def z_end(h):
        for j in outward(nz)[::-1]:
            frm = (z + nz - j) % nz
            remote(
                z_all.at[h, frm], z_all.at[h, frm], z_snd.at[h, j - 1], z_rcv.at[h, j - 1], ctx_z(frm), y
            ).wait_recv()
        total = z_all[h, 0].astype(F32)
        for k in range(1, nz):
            total += z_all[h, k].astype(F32)
        y_all[y, h] = total.astype(BF16)

    id_waits = []

    def send_ids():
        for j in range(1, ny):
            to, frm = (y + j) % ny, (y + ny - j) % ny
            copy = remote(ids_all.at[y], ids_all.at[y], id_snd.at[j - 1], id_rcv.at[j - 1], ctx, to)
            copy.start()
            sends.append(copy)
            id_waits.append(
                remote(ids_all.at[frm], ids_all.at[frm], id_snd.at[j - 1], id_rcv.at[j - 1], ctx, frm)
            )

    last = hx - 1
    send_edges(0)
    hear_word(1)
    for h in range(hx):
        for way in range(2):
            edge_copies[h, way].wait_recv()
        if h == 0:
            hear_word(2)
        compute(h)
        if h == 0:
            hear_word(3)
            send_ids()
        tables(h)
        send_back(h)
        if h < last:
            mains(h)
            send_edges(h + 1)
            hear_word(4)
            y_start(h)
    hear_word(5)
    for copy in id_waits:
        copy.wait_recv()
    for h in range(last):
        z_start(h)
    mains(last)
    y_start(last)
    for h in range(hx):
        send_dq(h)
    for h in range(hx):
        finish(h)
    z_start(last)
    for h in range(hx):
        z_end(h)

    def table_out(kind, yy, xs):
        return table.at[kind, xs, yy]

    for j in outward(ny)[::-1]:
        to = (y + j) % ny
        copy = remote(y_all.at[y], y_all.at[y], yg_snd.at[j - 1], yg_rcv.at[j - 1], ctx, to)
        copy.start()
        sends.append(copy)

    def to_sibling(src, yy, xs, j, d):
        copy = remote(src, table_out(c, yy, xs), cg_snd.at[j, d], cg_rcv.at[j, d], sib, y)
        copy.start()
        sends.append(copy)
        pending.append(
            remote(src, table_out(1 - c, yy, xs), cg_snd.at[j, d], cg_rcv.at[j, d], sib, y)
        )

    def spread(d):
        yy = (y + ny - d) % ny
        for j in (2, 1, 3):
            copy = remote(
                y_all.at[yy],
                table_out(c, yy, x),
                xg_snd.at[j - 1, d],
                xg_rcv.at[j - 1, d],
                ctx_x(at_x(j)),
                y,
            )
            copy.start()
            sends.append(copy)
        to_sibling(y_all.at[yy], yy, x, 0, d)
        copy = pltpu.make_async_copy(y_all.at[yy], table_out(c, yy, x), xg_loc.at[d])
        copy.start()
        locals_out.append(copy)

    def pass_on(d):
        yy = (y + ny - d) % ny
        for j in (1, 3, 2):
            frm = at_x(NX - j)
            remote(
                y_all.at[yy],
                table_out(c, yy, frm),
                xg_snd.at[j - 1, d],
                xg_rcv.at[j - 1, d],
                ctx_x(frm),
                y,
            ).wait_recv()
            to_sibling(table_out(c, yy, frm), yy, frm, j, d)

    spread(0)
    before = [0]
    near = outward(ny)[::-1]
    for start in range(0, len(near), 2):
        group = near[start : start + 2]
        for d in group:
            frm = (y + ny - d) % ny
            remote(
                y_all.at[frm], y_all.at[frm], yg_snd.at[d - 1], yg_rcv.at[d - 1], ctx, frm
            ).wait_recv()
            spread(d)
        for d in before:
            pass_on(d)
        before = group
    for d in before:
        pass_on(d)

    for copy in locals_out:
        copy.wait()
    final = [pltpu.make_async_copy(table.at[k], dg_out.at[k], t_out.at[i]) for i, k in enumerate((c, 1 - c))]
    final[0].start()
    for copy in pending:
        copy.wait_recv()
    final[1].start()
    for copy in sends:
        copy.wait_send()
    for copy in final:
        copy.wait()


def last_step(dq_in, dk_in, dv_in, dg_in, dq_out, dk_out, dv_out, dg_out, rows, narrow, full, got, put):
    parts = narrow.shape[0]
    loads = []
    for i in range(parts):
        loads.append(
            pltpu.make_async_copy(dg_in.at[i // NX, i % NX], narrow.at[i], got.at[i])
        )
    for i, src in enumerate((dq_in, dk_in, dv_in)):
        loads.append(pltpu.make_async_copy(src.at[0], rows.at[i], got.at[parts + i]))
    for copy in loads:
        copy.start()
    stores = []
    for i in range(parts):
        loads[i].wait()
        for h in range(narrow.shape[2]):
            for b in range(TABLE):
                rows_b = narrow[i, :, h, b].astype(F32).reshape(BLK, HS)
                full[i, b, :, h * HS : (h + 1) * HS] = rows_b
        cols = pl.ds(i % NX * full.shape[3], full.shape[3])
        copy = pltpu.make_async_copy(full.at[i], dg_out.at[i // NX, :, :, cols], put.at[i])
        copy.start()
        stores.append(copy)
    for i, dst_ref in enumerate((dq_out, dk_out, dv_out)):
        loads[parts + i].wait()
        copy = pltpu.make_async_copy(rows.at[i], dst_ref.at[0], put.at[parts + i])
        copy.start()
        stores.append(copy)
    for copy in stores:
        copy.wait()


def on_device(nz, ny, query, key, value, dout, glob_keys, glob_values, glob_ids, rand_blocks):
    heads = rand_blocks.shape[0]
    hx = heads // NX
    hd = query.shape[2]
    wide = hx * HS
    rows_y = BLK // ny
    blocks = [a.reshape(2, BLK, hd) for a in (query, key, value, dout)]
    rand = jnp.transpose(rand_blocks, (2, 0, 1))
    vm = pltpu.VMEM
    dma = pltpu.SemaphoreType.DMA
    out = jax.ShapeDtypeStruct((2, BLK, hd), BF16)
    anywhere = pl.BlockSpec(memory_space=pltpu.HBM)
    scalars = pl.BlockSpec(memory_space=pltpu.SMEM)
    scratch = [
        vm((hx, 2 * NX, 2, BLK, HS), BF16),
        vm((hx, 2 * NX, 2, BLK, HS), BF16),
        vm((hx, 2, 2 * NX, BLK, HS), BF16),
        vm((2, TABLE, BLK, wide), BF16),
        vm((hx, 2, 2, BLK, HS), BF16),
        vm((10 * BLK, NX * 2 * BLK), BF16),
        vm((10 * BLK, NX * 2 * BLK), BF16),
        vm((hx, NX, 2, BLK, HS), BF16),
        vm((hx, 2 * NX, 2, BLK, HS), F32),
        vm((hx, 2 * NX, 2, BLK, HS), BF16),
        vm((hx, 2, 2 * NX, BLK, HS), BF16),
        vm((hx, 2, 2 * NX, BLK, HS), BF16),
        vm((hx, 2, 2, BLK, HS), F32),
        vm((hx, 2, 2, BLK, HS), BF16),
        vm((hx, 2, BLK, HS), BF16),
        vm((ny, 2, rows_y, HS), jnp.int32),
        vm((hx, ny, 2, rows_y, HS), BF16),
        vm((hx, ny, 2, rows_y, HS), BF16),
        vm((hx, nz, TABLE, rows_y, HS), BF16),
        vm((ny, hx, TABLE, rows_y, HS), BF16),
        vm((2, NX, ny, hx, TABLE, rows_y, HS), BF16),
        dma((hx, 4)),
        dma((hx, 4, 3)),
        dma((hx, 4, 3)),
        dma((2,)),
        dma((hx, 2)),
        dma((hx, 2)),
        dma((hx, 2)),
        dma((hx, 2)),
        dma((hx,)),
        dma((hx, 3)),
        dma((hx, 3)),
        dma((hx, 2)),
        dma((hx, 2, 3)),
        dma((hx, 2, 3)),
        dma((hx,)),
        dma((hx,)),
        dma((ny,)),
        dma((ny,)),
        dma((hx, ny)),
        dma((hx, ny)),
        dma((hx, nz)),
        dma((hx, nz)),
        dma((ny,)),
        dma((ny,)),
        dma((ny,)),
        dma((2,)),
        dma((3, ny)),
        dma((3, ny)),
        dma((4, ny)),
        dma((4, ny)),
        pltpu.SemaphoreType.REGULAR((max(ny, nz) // 2, 4)),
    ]
    dq, dk, dv, dg = pl.pallas_call(
        functools.partial(body, nz, ny, hx),
        out_shape=(out, out, out, jax.ShapeDtypeStruct((2, NX, ny, hx, TABLE, rows_y, HS), BF16)),
        in_specs=[scalars, scalars] + [anywhere] * 6,
        out_specs=(anywhere,) * 4,
        scratch_shapes=scratch,
        compiler_params=pltpu.CompilerParams(
            collective_id=0, has_side_effects=True, vmem_limit_bytes=60 * 1024 * 1024
        ),
    )(glob_ids, rand, *blocks, glob_keys, glob_values)
    rows = jax.ShapeDtypeStruct((1, 2 * BLK, hd), BF16)
    dq, dk, dv = (a.reshape(1, 2 * BLK, hd) for a in (dq, dk, dv))
    parts = 2 * NX
    return tuple(
        pl.pallas_call(
            last_step,
            out_shape=(rows, rows, rows, jax.ShapeDtypeStruct((2, TABLE, BLK, hd), F32)),
            in_specs=[anywhere] * 4,
            out_specs=(anywhere,) * 4,
            scratch_shapes=[
                vm((3, 2 * BLK, hd), BF16),
                vm((parts, ny, hx, TABLE, rows_y, HS), BF16),
                vm((parts, TABLE, BLK, wide), F32),
                dma((parts + 3,)),
                dma((parts + 3,)),
            ],
            compiler_params=pltpu.CompilerParams(vmem_limit_bytes=60 * 1024 * 1024),
        )(dq, dk, dv, dg)
    )


def solution(mesh):
    ny = mesh.shape["dp"]
    nz = mesh.shape["ctx"] // (2 * NX)
    split = P("dp", "ctx", None)
    return jax.shard_map(
        functools.partial(on_device, nz, ny),
        mesh=mesh,
        in_specs=(split, split, split, split, P(), P(), P("dp", None), P()),
        out_specs=(split, split, split, P()),
        check_vma=False,
    )
```

```python
import functools
import math

import jax
import jax.numpy as jnp
from jax import lax
from jax.experimental import pallas as pl
from jax.experimental.pallas import tpu as pltpu
from jax.sharding import PartitionSpec as P

BLK = 64
HS = 128
NX = 4
SLOTS = 3
TABLE = 4
MESH = pl.DeviceIdType.MESH
BF16 = jnp.bfloat16
F32 = jnp.float32


def dot_nt(a, b):
    return lax.dot_general(a, b, (((1,), (1,)), ((), ())), preferred_element_type=F32)


def dot_nn(a, b):
    return lax.dot_general(a, b, (((1,), (0,)), ((), ())), preferred_element_type=F32)


def dot_tn(a, b):
    return lax.dot_general(a, b, (((0,), (0,)), ((), ())), preferred_element_type=F32)


def outward(count):
    return sorted(range(1, count), key=lambda j: (-min(j, count - j), j))


def body(
    nz,
    ny,
    hx,
    ids_in,
    rand_in,
    q_in,
    k_in,
    v_in,
    o_in,
    gk_in,
    gv_in,
    dq_out,
    dk_out,
    dv_out,
    dg_out,
    kv,
    qd,
    edge,
    tab,
    gsel,
    pt,
    dst,
    dqs,
    dkv,
    dkvb,
    edge_s,
    edge_r,
    gp,
    gpb,
    g_core,
    ids_all,
    y_send,
    y_recv,
    z_all,
    y_all,
    table,
    in_loc,
    in_snd,
    in_rcv,
    tab_sem,
    e_snd,
    e_rcv,
    b_snd,
    b_rcv,
    dq_loc,
    dq_snd,
    dq_rcv,
    dkv_loc,
    dkv_snd,
    dkv_rcv,
    c_snd,
    c_rcv,
    id_snd,
    id_rcv,
    yr_snd,
    yr_rcv,
    z_snd,
    z_rcv,
    yg_snd,
    yg_rcv,
    xg_loc,
    t_out,
    xg_snd,
    xg_rcv,
    cg_snd,
    cg_rcv,
    word,
    ids_ref,
    rand_ref,
    scalar_sem,
):
    ring = nz * 2
    ctx = lax.axis_index("ctx")
    y = lax.axis_index("dp")
    x = ctx // ring
    pos = ctx % ring
    z = pos // 2
    c = pos % 2
    wide = hx * HS
    scaling = 1.0 / math.sqrt(HS)
    own_cols = pl.multiple_of(x * wide, HS)
    up = x * ring + (pos + 1) % ring
    low = x * ring + (pos + ring - 1) % ring
    sib = x * ring + z * 2 + (1 - c)
    far = x * ring + jnp.where(c == 0, (pos + ring - 1) % ring, (pos + 1) % ring)

    def at_x(step):
        return (x + step) % NX

    def ctx_x(xs):
        return xs * ring + pos

    def ctx_z(zs):
        return x * ring + zs * 2 + c

    def remote(src, dst_ref, snd, rcv, to_ctx, to_y):
        return pltpu.make_async_remote_copy(
            src_ref=src,
            dst_ref=dst_ref,
            send_sem=snd,
            recv_sem=rcv,
            device_id={"ctx": to_ctx, "dp": to_y},
            device_id_type=MESH,
        )

    scalar_copies = []
    for i, (src, dst_ref) in enumerate(((ids_in, ids_ref), (rand_in, rand_ref))):
        copy = pltpu.make_async_copy(src, dst_ref, scalar_sem.at[i])
        copy.start()
        scalar_copies.append(copy)
    tab_copies = []
    for t, blocks in enumerate((gk_in, gv_in)):
        copy = pltpu.make_async_copy(blocks.at[:, :, pl.ds(own_cols, wide)], tab.at[t], tab_sem.at[t])
        copy.start()
        tab_copies.append(copy)

    tensors = (k_in, v_in, q_in, o_in)

    def land(h, t, xs):
        return (kv if t < 2 else qd).at[h, (t % 2) * NX + xs]

    local_in = {}
    for t in range(4):
        for h in range(hx):
            copy = pltpu.make_async_copy(
                tensors[t].at[:, :, pl.ds(pl.multiple_of(x * wide + h * HS, HS), HS)],
                land(h, t, x),
                in_loc.at[h, t],
            )
            copy.start()
            local_in[h, t] = copy

    beside = [(ctx, (y + 1) % ny), (ctx, (y + ny - 1) % ny)]
    beside += [(ctx_z((z + 1) % nz), y), (ctx_z((z + nz - 1) % nz), y)]

    def pass_word(k):
        for i, (to_ctx, to_y) in enumerate(beside):
            if k <= (ny if i < 2 else nz) // 2 - 1:
                pl.semaphore_signal(
                    word.at[k - 1, i], inc=1, device_id={"ctx": to_ctx, "dp": to_y}, device_id_type=MESH
                )

    def hear_word(k):
        for i in range(4):
            if k <= (ny if i < 2 else nz) // 2 - 1:
                pl.semaphore_wait(word.at[k - 1, i], 1)
        pass_word(k + 1)

    barrier = pltpu.get_barrier_semaphore()
    partners = [(ctx_x(at_x(j)), y) for j in range(1, NX)]
    partners += [(sib, y), (far, y)]
    partners += beside
    for to_ctx, to_y in partners:
        pl.semaphore_signal(barrier, inc=1, device_id={"ctx": to_ctx, "dp": to_y}, device_id_type=MESH)
    pl.semaphore_wait(barrier, len(partners))
    pass_word(1)

    sends = []

    def send_in(h, t, j):
        to = at_x(j)
        copy = remote(
            tensors[t].at[:, :, pl.ds(pl.multiple_of(to * wide + h * HS, HS), HS)],
            land(h, t, x),
            in_snd.at[h, t, j - 1],
            in_rcv.at[h, t, j - 1],
            ctx_x(to),
            y,
        )
        copy.start()
        sends.append(copy)

    def wait_in(h, t):
        local_in[h, t].wait()
        for j in (1, 3, 2):
            frm = at_x(NX - j)
            remote(
                land(h, t, frm), land(h, t, frm), in_snd.at[h, t, j - 1], in_rcv.at[h, t, j - 1], ctx_x(frm), y
            ).wait_recv()

    for h in range(hx):
        for t in range(2):
            for j in (2, 1, 3):
                send_in(h, t, j)
    for h in range(hx):
        for j in (1, 3, 2):
            for t in range(2, 4):
                send_in(h, t, j)

    for copy in scalar_copies:
        copy.wait()

    for s in range(2):
        ids_all[y, s] = jnp.full((BLK // ny, HS), ids_ref[0, s], jnp.int32)
    for copy in tab_copies:
        copy.wait()
    for h in range(hx):
        for t in range(2):
            for s in range(2):
                gsel[h, t, s] = tab[t, ids_ref[0, s], :, h * HS : (h + 1) * HS]

    edge_copies = {}


    def send_edges(h):
        wait_in(h, 0)
        wait_in(h, 1)
        for way, to in ((0, up), (1, low)):
            copy = remote(
                kv.at[h, :, 1 - way], edge.at[h, way], e_snd.at[h, way], e_rcv.at[h, way], to, y
            )
            copy.start()
            edge_copies[h, way] = copy
            sends.append(copy)

    seam_low = jnp.where(pos == 0, 1, 0)
    seam_up = jnp.where(pos == ring - 1, 1, 0)

    def compute(h):
        k_main = kv[h, 0:NX].reshape(NX * 2 * BLK, HS)
        v_main = kv[h, NX : 2 * NX].reshape(NX * 2 * BLK, HS)
        k_tab = gsel[h, 0].reshape(2 * BLK, HS)
        v_tab = gsel[h, 1].reshape(2 * BLK, HS)
        lane = lax.broadcasted_iota(jnp.int32, (1, 2 * BLK), 1)
        half = lane // BLK

        def span(i, carry):
            off = jnp.where(i == 1, NX - 1, jnp.where(i == 0, 0, i - 1))
            xq = (x + off) % NX
            sem = jnp.where(i == 1, 0, jnp.where(i == 2, 2, 1))

            @pl.when(i > 0)
            def _():
                for t in range(2, 4):
                    remote(
                        land(h, t, xq), land(h, t, xq), in_snd.at[h, t, sem], in_rcv.at[h, t, sem], ctx_x(xq), y
                    ).wait_recv()

            q = qd[h, xq].reshape(2 * BLK, HS)
            g = qd[h, NX + xq].reshape(2 * BLK, HS)
            i_low = (xq + NX - seam_low) % NX
            i_up = (xq + seam_up) % NX
            k_edge = jnp.concatenate([edge[h, 0, i_low], edge[h, 1, i_up]], axis=0)
            v_edge = jnp.concatenate([edge[h, 0, NX + i_low], edge[h, 1, NX + i_up]], axis=0)
            s_main = dot_nt(k_main, q)
            s_tab = dot_nt(k_tab, q)
            s_edge = dot_nt(k_edge, q)
            block = 2 * (xq * ring + pos)
            pieces = []
            for xs in range(NX):
                slot = (xs + NX - xq - 1) % NX
                row = jnp.minimum(slot, SLOTS - 1)
                first = rand_ref[row, x * hx + h, block] % 2
                second = rand_ref[row, x * hx + h, block + 1] % 2
                own = jnp.where(slot == SLOTS, 1, 0)
                inside = jnp.where(half == 0, first, second)
                for b in range(2):
                    hit = jnp.where(inside == b, 1, own)
                    keep = jnp.broadcast_to(hit, (BLK, 2 * BLK)) > 0
                    at = (xs * 2 + b) * BLK
                    pieces.append(jnp.where(keep, s_main[at : at + BLK], -1e30))
            pieces += [s_tab[:BLK], s_tab[BLK:]]
            ok_low = jnp.where(jnp.logical_and(xq == 0, pos == 0), 0, 1)
            ok_up = jnp.where(jnp.logical_and(xq == NX - 1, pos == ring - 1), 0, 1)
            for b, ok in ((0, ok_low), (1, ok_up)):
                hit = jnp.where(half == b, ok, 0)
                keep = jnp.broadcast_to(hit, (BLK, 2 * BLK)) > 0
                pieces.append(jnp.where(keep, s_edge[b * BLK : (b + 1) * BLK], -1e30))
            top = functools.reduce(jnp.maximum, pieces)
            top = jnp.max(top, axis=0, keepdims=True)
            exps = [jnp.exp2((piece - top) * (scaling * math.log2(math.e))) for piece in pieces]
            total = jnp.sum(functools.reduce(jnp.add, exps), axis=0, keepdims=True)
            inverse = 1.0 / total
            d_main = dot_nt(v_main, g)
            d_tab = dot_nt(v_tab, g)
            d_edge = dot_nt(v_edge, g)
            d_pieces = [d_main[i * BLK : (i + 1) * BLK] for i in range(2 * NX)]
            d_pieces += [d_tab[:BLK], d_tab[BLK:], d_edge[:BLK], d_edge[BLK:]]
            probs = [e * inverse for e in exps]
            probs_b = [p.astype(BF16) for p in probs]
            dots = functools.reduce(
                jnp.add, [p.astype(F32) * d for p, d in zip(probs_b, d_pieces)]
            )
            row_dot = jnp.sum(dots, axis=0, keepdims=True)
            grads = [
                (p * (d - row_dot) * scaling).astype(BF16) for p, d in zip(probs, d_pieces)
            ]
            cols = pl.ds(pl.multiple_of(xq * 2 * BLK, 2 * BLK), 2 * BLK)
            pt[:, cols] = jnp.concatenate(probs_b, axis=0)
            dst[:, cols] = jnp.concatenate(grads, axis=0)
            return carry

        for t in range(2, 4):
            local_in[h, t].wait()
        lax.fori_loop(0, NX, span, 0)

    last_row = NX * 2 * BLK
    tab_row = last_row + 2 * BLK

    def tables(h):
        for t, lists in ((0, dst), (1, pt)):
            rows = qd[h, t * NX : (t + 1) * NX].reshape(NX * 2 * BLK, HS)
            grad = dot_nn(lists[last_row:tab_row], rows).reshape(2, BLK, HS)
            gp[h, t] = grad
            gpb[h, t] = grad.astype(BF16)
        copy = remote(gpb.at[h, 1 - c], g_core.at[h], c_snd.at[h], c_rcv.at[h], sib, y)
        copy.start()
        core_copies[h] = copy
        sends.append(copy)

    def edges_of(h, t, xs):
        i_low = (xs + NX - seam_low) % NX + t * NX
        i_up = (xs + seam_up) % NX + t * NX
        return jnp.concatenate([edge[h, 0, i_low], edge[h, 1, i_up]], axis=0), i_low, i_up

    def mains(h):
        dq = dot_tn(dst[:last_row], kv[h, 0:NX].reshape(last_row, HS))
        dq += dot_tn(dst[last_row:tab_row], gsel[h, 0].reshape(2 * BLK, HS))
        for xs in range(NX):
            part = slice(xs * 2 * BLK, (xs + 1) * 2 * BLK)
            k_edge = edges_of(h, 0, xs)[0]
            dq_edge = dot_tn(dst[tab_row:, part], k_edge)
            dqs[h, xs] = (dq[part] + dq_edge).astype(BF16).reshape(2, BLK, HS)
            for t, lists in ((0, dst), (1, pt)):
                rows = qd[h, t * NX + xs].reshape(2 * BLK, HS)
                grad = dot_nn(lists[tab_row:, part], rows).astype(BF16)
                _, i_low, i_up = edges_of(h, t, xs)
                edge_s[h, 0, i_low] = grad[:BLK]
                edge_s[h, 1, i_up] = grad[BLK:]
        for t, lists in ((0, dst), (1, pt)):
            rows = qd[h, t * NX : (t + 1) * NX].reshape(NX * 2 * BLK, HS)
            grad = dot_nn(lists[:last_row], rows)
            dkv[h, t * NX : (t + 1) * NX] = grad.reshape(NX, 2, BLK, HS)

    core_copies = {}
    back_copies = {}
    pending = []
    locals_out = []

    def out_cols(xs, h):
        return pl.ds(pl.multiple_of(xs * wide + h * HS, HS), HS)

    def send_out(out, src_of, h, snd, rcv, loc):
        for j in (2, 1, 3):
            to = at_x(j)
            copy = remote(
                src_of(to), out.at[:, :, out_cols(x, h)], snd(j - 1), rcv(j - 1), ctx_x(to), y
            )
            copy.start()
            sends.append(copy)
            frm = at_x(NX - j)
            pending.append(
                remote(
                    src_of(to), out.at[:, :, out_cols(frm, h)], snd(j - 1), rcv(j - 1), ctx_x(to), y
                )
            )
        copy = pltpu.make_async_copy(src_of(x), out.at[:, :, out_cols(x, h)], loc)
        copy.start()
        locals_out.append(copy)

    def send_back(h):
        for way, to in ((0, low), (1, up)):
            copy = remote(
                edge_s.at[h, way], edge_r.at[h, way], b_snd.at[h, way], b_rcv.at[h, way], to, y
            )
            copy.start()
            back_copies[h, way] = copy
            sends.append(copy)

    def send_dq(h):
        send_out(
            dq_out,
            lambda xs: dqs.at[h, xs],
            h,
            lambda j: dq_snd.at[h, j],
            lambda j: dq_rcv.at[h, j],
            dq_loc.at[h],
        )

    def finish(h):
        for way in range(2):
            back_copies[h, way].wait_recv()
        for t in range(2):
            for b in range(2):
                part = slice(t * NX, (t + 1) * NX)
                total = dkv[h, part, b] + edge_r[h, 1 - b, part].astype(F32)
                dkvb[h, part, b] = total.astype(BF16)
        for t, out in ((0, dk_out), (1, dv_out)):
            send_out(
                out,
                lambda xs, t=t: dkvb.at[h, t * NX + xs],
                h,
                lambda j, t=t: dkv_snd.at[h, t, j],
                lambda j, t=t: dkv_rcv.at[h, t, j],
                dkv_loc.at[h, t],
            )

    rows_y = BLK // ny

    def y_start(h):
        core_copies[h].wait_recv()
        for s in range(2):
            both = (gp[h, c, s] + g_core[h, s].astype(F32)).astype(BF16)
            for r in range(ny):
                y_send[h, r, s] = both[r * rows_y : (r + 1) * rows_y]
        for j in outward(ny):
            to = (y + j) % ny
            copy = remote(
                y_send.at[h, to], y_recv.at[h, y], yr_snd.at[h, j - 1], yr_rcv.at[h, j - 1], ctx, to
            )
            copy.start()
            sends.append(copy)
        y_recv[h, y] = y_send[h, y]

    def z_start(h):
        for j in outward(ny)[::-1]:
            frm = (y + ny - j) % ny
            remote(
                y_send.at[h, y], y_recv.at[h, frm], yr_snd.at[h, j - 1], yr_rcv.at[h, j - 1], ctx, frm
            ).wait_recv()
        sums = [jnp.zeros((rows_y, HS), F32) for _ in range(TABLE)]
        for src in range(ny):
            for s in range(2):
                chosen = ids_all[src, s]
                term = y_recv[h, src, s].astype(F32)
                sums = [acc + jnp.where(chosen == b, term, 0.0) for b, acc in enumerate(sums)]
        for b in range(TABLE):
            z_all[h, z, b] = sums[b].astype(BF16)
        for j in outward(nz):
            to = (z + j) % nz
            copy = remote(
                z_all.at[h, z], z_all.at[h, z], z_snd.at[h, j - 1], z_rcv.at[h, j - 1], ctx_z(to), y
            )
            copy.start()
            sends.append(copy)

    def z_end(h):
        for j in outward(nz)[::-1]:
            frm = (z + nz - j) % nz
            remote(
                z_all.at[h, frm], z_all.at[h, frm], z_snd.at[h, j - 1], z_rcv.at[h, j - 1], ctx_z(frm), y
            ).wait_recv()
        total = z_all[h, 0].astype(F32)
        for k in range(1, nz):
            total += z_all[h, k].astype(F32)
        y_all[y, h] = total.astype(BF16)

    id_waits = []

    def send_ids():
        for j in range(1, ny):
            to, frm = (y + j) % ny, (y + ny - j) % ny
            copy = remote(ids_all.at[y], ids_all.at[y], id_snd.at[j - 1], id_rcv.at[j - 1], ctx, to)
            copy.start()
            sends.append(copy)
            id_waits.append(
                remote(ids_all.at[frm], ids_all.at[frm], id_snd.at[j - 1], id_rcv.at[j - 1], ctx, frm)
            )

    last = hx - 1
    for h in range(hx):
        send_edges(h)
    hear_word(1)
    for h in range(hx):
        for way in range(2):
            edge_copies[h, way].wait_recv()
        if h == 0:
            hear_word(2)
        compute(h)
        if h == 0:
            hear_word(3)
            send_ids()
        tables(h)
        if h < last:
            mains(h)
            send_back(h)
            hear_word(4)
            y_start(h)
    hear_word(5)
    for copy in id_waits:
        copy.wait_recv()
    for h in range(last):
        z_start(h)
    y_start(last)
    mains(last)
    send_back(last)
    for h in range(hx):
        send_dq(h)
    for h in range(last):
        finish(h)
    z_start(last)
    finish(last)
    for h in range(hx):
        z_end(h)

    def table_out(kind, yy, xs):
        return table.at[kind, xs, yy]

    for j in outward(ny)[::-1]:
        to = (y + j) % ny
        copy = remote(y_all.at[y], y_all.at[y], yg_snd.at[j - 1], yg_rcv.at[j - 1], ctx, to)
        copy.start()
        sends.append(copy)

    def to_sibling(src, yy, xs, j, d):
        copy = remote(src, table_out(c, yy, xs), cg_snd.at[j, d], cg_rcv.at[j, d], sib, y)
        copy.start()
        sends.append(copy)
        pending.append(
            remote(src, table_out(1 - c, yy, xs), cg_snd.at[j, d], cg_rcv.at[j, d], sib, y)
        )

    def spread(d):
        yy = (y + ny - d) % ny
        for j in (2, 1, 3):
            copy = remote(
                y_all.at[yy],
                table_out(c, yy, x),
                xg_snd.at[j - 1, d],
                xg_rcv.at[j - 1, d],
                ctx_x(at_x(j)),
                y,
            )
            copy.start()
            sends.append(copy)
        to_sibling(y_all.at[yy], yy, x, 0, d)
        copy = pltpu.make_async_copy(y_all.at[yy], table_out(c, yy, x), xg_loc.at[d])
        copy.start()
        locals_out.append(copy)

    def pass_on(d):
        yy = (y + ny - d) % ny
        for j in (1, 3, 2):
            frm = at_x(NX - j)
            remote(
                y_all.at[yy],
                table_out(c, yy, frm),
                xg_snd.at[j - 1, d],
                xg_rcv.at[j - 1, d],
                ctx_x(frm),
                y,
            ).wait_recv()
            to_sibling(table_out(c, yy, frm), yy, frm, j, d)

    spread(0)
    before = [0]
    near = outward(ny)[::-1]
    for start in range(0, len(near), 2):
        group = near[start : start + 2]
        for d in group:
            frm = (y + ny - d) % ny
            remote(
                y_all.at[frm], y_all.at[frm], yg_snd.at[d - 1], yg_rcv.at[d - 1], ctx, frm
            ).wait_recv()
            spread(d)
        for d in before:
            pass_on(d)
        before = group
    for d in before:
        pass_on(d)

    for copy in locals_out:
        copy.wait()
    final = [pltpu.make_async_copy(table.at[k], dg_out.at[k], t_out.at[i]) for i, k in enumerate((c, 1 - c))]
    final[0].start()
    for copy in pending:
        copy.wait_recv()
    final[1].start()
    for copy in sends:
        copy.wait_send()
    for copy in final:
        copy.wait()


def last_step(dq_in, dk_in, dv_in, dg_in, dq_out, dk_out, dv_out, dg_out, full, put):
    kinds, parts, _, heads = dg_in.shape[:4]
    stores = []
    for kind in range(kinds):
        for xs in range(parts):
            i = kind * parts + xs
            for h in range(heads):
                for b in range(TABLE):
                    rows_b = dg_in[kind, xs, :, h, b].astype(F32).reshape(BLK, HS)
                    full[i, b, :, h * HS : (h + 1) * HS] = rows_b
            cols = pl.ds(xs * full.shape[3], full.shape[3])
            stores.append(
                pltpu.make_async_copy(full.at[i], dg_out.at[kind, :, :, cols], put.at[i])
            )
            stores[-1].start()
    for i, (src, dst_ref) in enumerate(((dq_in, dq_out), (dk_in, dk_out), (dv_in, dv_out))):
        stores.append(pltpu.make_async_copy(src, dst_ref, put.at[kinds * parts + i]))
        stores[-1].start()
    for copy in stores:
        copy.wait()


def on_device(nz, ny, query, key, value, dout, glob_keys, glob_values, glob_ids, rand_blocks):
    heads = rand_blocks.shape[0]
    hx = heads // NX
    hd = query.shape[2]
    wide = hx * HS
    rows_y = BLK // ny
    blocks = [a.reshape(2, BLK, hd) for a in (query, key, value, dout)]
    rand = jnp.transpose(rand_blocks, (2, 0, 1))
    operands = (glob_ids, rand, *blocks, glob_keys, glob_values)
    vm = pltpu.VMEM
    dma = pltpu.SemaphoreType.DMA
    out = jax.ShapeDtypeStruct((2, BLK, hd), BF16)
    anywhere = pl.BlockSpec(memory_space=pltpu.HBM)
    scratch = [
        vm((hx, 2 * NX, 2, BLK, HS), BF16),
        vm((hx, 2 * NX, 2, BLK, HS), BF16),
        vm((hx, 2, 2 * NX, BLK, HS), BF16),
        vm((2, TABLE, BLK, wide), BF16),
        vm((hx, 2, 2, BLK, HS), BF16),
        vm((12 * BLK, NX * 2 * BLK), BF16),
        vm((12 * BLK, NX * 2 * BLK), BF16),
        vm((hx, NX, 2, BLK, HS), BF16),
        vm((hx, 2 * NX, 2, BLK, HS), F32),
        vm((hx, 2 * NX, 2, BLK, HS), BF16),
        vm((hx, 2, 2 * NX, BLK, HS), BF16),
        vm((hx, 2, 2 * NX, BLK, HS), BF16),
        vm((hx, 2, 2, BLK, HS), F32),
        vm((hx, 2, 2, BLK, HS), BF16),
        vm((hx, 2, BLK, HS), BF16),
        vm((ny, 2, rows_y, HS), jnp.int32),
        vm((hx, ny, 2, rows_y, HS), BF16),
        vm((hx, ny, 2, rows_y, HS), BF16),
        vm((hx, nz, TABLE, rows_y, HS), BF16),
        vm((ny, hx, TABLE, rows_y, HS), BF16),
        vm((2, NX, ny, hx, TABLE, rows_y, HS), BF16),
        dma((hx, 4)),
        dma((hx, 4, 3)),
        dma((hx, 4, 3)),
        dma((2,)),
        dma((hx, 2)),
        dma((hx, 2)),
        dma((hx, 2)),
        dma((hx, 2)),
        dma((hx,)),
        dma((hx, 3)),
        dma((hx, 3)),
        dma((hx, 2)),
        dma((hx, 2, 3)),
        dma((hx, 2, 3)),
        dma((hx,)),
        dma((hx,)),
        dma((ny,)),
        dma((ny,)),
        dma((hx, ny)),
        dma((hx, ny)),
        dma((hx, nz)),
        dma((hx, nz)),
        dma((ny,)),
        dma((ny,)),
        dma((ny,)),
        dma((2,)),
        dma((3, ny)),
        dma((3, ny)),
        dma((4, ny)),
        dma((4, ny)),
        pltpu.SemaphoreType.REGULAR((max(ny, nz) // 2, 4)),
        pltpu.SMEM(glob_ids.shape, jnp.int32),
        pltpu.SMEM(rand.shape, jnp.int32),
        dma((2,)),
    ]
    dq, dk, dv, dg = pl.pallas_call(
        functools.partial(body, nz, ny, hx),
        out_shape=(out, out, out, jax.ShapeDtypeStruct((2, NX, ny, hx, TABLE, rows_y, HS), BF16)),
        in_specs=[pl.BlockSpec(memory_space=pltpu.HBM)] * 8,
        out_specs=(anywhere,) * 4,
        scratch_shapes=scratch,
        compiler_params=pltpu.CompilerParams(
            collective_id=0, has_side_effects=True, vmem_limit_bytes=40 * 1024 * 1024
        ),
    )(*[pltpu.with_memory_space_constraint(a, pltpu.HBM) for a in operands])
    rows = jax.ShapeDtypeStruct((1, 2 * BLK, hd), BF16)
    dq, dk, dv = (a.reshape(1, 2 * BLK, hd) for a in (dq, dk, dv))
    parts = 2 * NX
    return tuple(
        pl.pallas_call(
            last_step,
            out_shape=(rows, rows, rows, jax.ShapeDtypeStruct((2, TABLE, BLK, hd), F32)),
            in_specs=[pl.BlockSpec(memory_space=pltpu.VMEM)] * 4,
            out_specs=(anywhere,) * 4,
            scratch_shapes=[
                vm((parts, TABLE, BLK, wide), F32),
                dma((parts + 3,)),
            ],
            compiler_params=pltpu.CompilerParams(vmem_limit_bytes=16 * 1024 * 1024),
        )(dq, dk, dv, dg)
    )


def solution(mesh):
    ny = mesh.shape["dp"]
    nz = mesh.shape["ctx"] // (2 * NX)
    split = P("dp", "ctx", None)
    return jax.shard_map(
        functools.partial(on_device, nz, ny),
        mesh=mesh,
        in_specs=(split, split, split, split, P(), P(), P("dp", None), P()),
        out_specs=(split, split, split, P()),
        check_vma=False,
    )
```

```python
import functools
import math

import jax
import jax.numpy as jnp
from jax import lax
from jax.experimental import pallas as pl
from jax.experimental.pallas import tpu as pltpu
from jax.sharding import PartitionSpec as P

BLK = 64
HS = 128
NX = 4
SLOTS = 3
TABLE = 4
MESH = pl.DeviceIdType.MESH
BF16 = jnp.bfloat16
F32 = jnp.float32


def dot_nt(a, b):
    return lax.dot_general(a, b, (((1,), (1,)), ((), ())), preferred_element_type=F32)


def dot_nn(a, b):
    return lax.dot_general(a, b, (((1,), (0,)), ((), ())), preferred_element_type=F32)


def dot_tn(a, b):
    return lax.dot_general(a, b, (((0,), (0,)), ((), ())), preferred_element_type=F32)


def outward(count):
    return sorted(range(1, count), key=lambda j: (-min(j, count - j), j))


def body(
    nz,
    ny,
    hx,
    ids_in,
    rand_in,
    q_in,
    k_in,
    v_in,
    o_in,
    gk_in,
    gv_in,
    dq_out,
    dk_out,
    dv_out,
    dg_out,
    kv,
    qd,
    edge,
    tab,
    gsel,
    pt,
    dst,
    dqs,
    dkv,
    dkvb,
    edge_s,
    edge_r,
    gp,
    gpb,
    g_core,
    ids_all,
    y_send,
    y_recv,
    z_all,
    y_all,
    in_loc,
    in_snd,
    in_rcv,
    tab_sem,
    e_snd,
    e_rcv,
    b_snd,
    b_rcv,
    dq_loc,
    dq_snd,
    dq_rcv,
    dkv_loc,
    dkv_snd,
    dkv_rcv,
    c_snd,
    c_rcv,
    id_snd,
    id_rcv,
    yr_snd,
    yr_rcv,
    z_snd,
    z_rcv,
    yg_snd,
    yg_rcv,
    xg_loc,
    xg_snd,
    xg_rcv,
    cg_snd,
    cg_rcv,
    word,
    ids_ref,
    rand_ref,
    scalar_sem,
):
    ring = nz * 2
    ctx = lax.axis_index("ctx")
    y = lax.axis_index("dp")
    x = ctx // ring
    pos = ctx % ring
    z = pos // 2
    c = pos % 2
    wide = hx * HS
    scaling = 1.0 / math.sqrt(HS)
    own_cols = pl.multiple_of(x * wide, HS)
    up = x * ring + (pos + 1) % ring
    low = x * ring + (pos + ring - 1) % ring
    sib = x * ring + z * 2 + (1 - c)
    far = x * ring + jnp.where(c == 0, (pos + ring - 1) % ring, (pos + 1) % ring)

    def at_x(step):
        return (x + step) % NX

    def ctx_x(xs):
        return xs * ring + pos

    def ctx_z(zs):
        return x * ring + zs * 2 + c

    def remote(src, dst_ref, snd, rcv, to_ctx, to_y):
        return pltpu.make_async_remote_copy(
            src_ref=src,
            dst_ref=dst_ref,
            send_sem=snd,
            recv_sem=rcv,
            device_id={"ctx": to_ctx, "dp": to_y},
            device_id_type=MESH,
        )

    scalar_copies = []
    for i, (src, dst_ref) in enumerate(((ids_in, ids_ref), (rand_in, rand_ref))):
        copy = pltpu.make_async_copy(src, dst_ref, scalar_sem.at[i])
        copy.start()
        scalar_copies.append(copy)
    tab_copies = []
    for t, blocks in enumerate((gk_in, gv_in)):
        copy = pltpu.make_async_copy(blocks.at[:, :, pl.ds(own_cols, wide)], tab.at[t], tab_sem.at[t])
        copy.start()
        tab_copies.append(copy)

    tensors = (k_in, v_in, q_in, o_in)

    def land(h, t, xs):
        return (kv if t < 2 else qd).at[h, (t % 2) * NX + xs]

    local_in = {}
    for t in range(4):
        for h in range(hx):
            copy = pltpu.make_async_copy(
                tensors[t].at[:, :, pl.ds(pl.multiple_of(x * wide + h * HS, HS), HS)],
                land(h, t, x),
                in_loc.at[h, t],
            )
            copy.start()
            local_in[h, t] = copy

    beside = [(ctx, (y + 1) % ny), (ctx, (y + ny - 1) % ny)]
    beside += [(ctx_z((z + 1) % nz), y), (ctx_z((z + nz - 1) % nz), y)]

    def pass_word(k):
        for i, (to_ctx, to_y) in enumerate(beside):
            if k <= (ny if i < 2 else nz) // 2 - 1:
                pl.semaphore_signal(
                    word.at[k - 1, i], inc=1, device_id={"ctx": to_ctx, "dp": to_y}, device_id_type=MESH
                )

    def hear_word(k):
        for i in range(4):
            if k <= (ny if i < 2 else nz) // 2 - 1:
                pl.semaphore_wait(word.at[k - 1, i], 1)
        pass_word(k + 1)

    barrier = pltpu.get_barrier_semaphore()
    partners = [(ctx_x(at_x(j)), y) for j in range(1, NX)]
    partners += [(sib, y), (far, y)]
    partners += beside
    for to_ctx, to_y in partners:
        pl.semaphore_signal(barrier, inc=1, device_id={"ctx": to_ctx, "dp": to_y}, device_id_type=MESH)
    pl.semaphore_wait(barrier, len(partners))
    pass_word(1)

    sends = []

    def send_in(h, t, j):
        to = at_x(j)
        copy = remote(
            tensors[t].at[:, :, pl.ds(pl.multiple_of(to * wide + h * HS, HS), HS)],
            land(h, t, x),
            in_snd.at[h, t, j - 1],
            in_rcv.at[h, t, j - 1],
            ctx_x(to),
            y,
        )
        copy.start()
        sends.append(copy)

    def wait_in(h, t):
        local_in[h, t].wait()
        for j in (1, 3, 2):
            frm = at_x(NX - j)
            remote(
                land(h, t, frm), land(h, t, frm), in_snd.at[h, t, j - 1], in_rcv.at[h, t, j - 1], ctx_x(frm), y
            ).wait_recv()

    for h in range(hx):
        for t in range(2):
            for j in (2, 1, 3):
                send_in(h, t, j)
    for h in range(hx):
        for j in (1, 3, 2):
            for t in range(2, 4):
                send_in(h, t, j)

    for copy in scalar_copies:
        copy.wait()

    for s in range(2):
        ids_all[y, s] = jnp.full((BLK // ny, HS), ids_ref[0, s], jnp.int32)
    for copy in tab_copies:
        copy.wait()
    for h in range(hx):
        for t in range(2):
            for s in range(2):
                gsel[h, t, s] = tab[t, ids_ref[0, s], :, h * HS : (h + 1) * HS]

    edge_copies = {}


    def send_edges(h):
        wait_in(h, 0)
        wait_in(h, 1)
        for way, to in ((0, up), (1, low)):
            copy = remote(
                kv.at[h, :, 1 - way], edge.at[h, way], e_snd.at[h, way], e_rcv.at[h, way], to, y
            )
            copy.start()
            edge_copies[h, way] = copy
            sends.append(copy)

    seam_low = jnp.where(pos == 0, 1, 0)
    seam_up = jnp.where(pos == ring - 1, 1, 0)

    def compute(h):
        k_main = kv[h, 0:NX].reshape(NX * 2 * BLK, HS)
        v_main = kv[h, NX : 2 * NX].reshape(NX * 2 * BLK, HS)
        k_tab = gsel[h, 0].reshape(2 * BLK, HS)
        v_tab = gsel[h, 1].reshape(2 * BLK, HS)
        lane = lax.broadcasted_iota(jnp.int32, (1, 2 * BLK), 1)
        half = lane // BLK

        def span(i, carry):
            off = jnp.where(i == 1, NX - 1, jnp.where(i == 0, 0, i - 1))
            xq = (x + off) % NX
            sem = jnp.where(i == 1, 0, jnp.where(i == 2, 2, 1))

            @pl.when(i > 0)
            def _():
                for t in range(2, 4):
                    remote(
                        land(h, t, xq), land(h, t, xq), in_snd.at[h, t, sem], in_rcv.at[h, t, sem], ctx_x(xq), y
                    ).wait_recv()

            q = qd[h, xq].reshape(2 * BLK, HS)
            g = qd[h, NX + xq].reshape(2 * BLK, HS)
            i_low = (xq + NX - seam_low) % NX
            i_up = (xq + seam_up) % NX
            k_edge = jnp.concatenate([edge[h, 0, i_low], edge[h, 1, i_up]], axis=0)
            v_edge = jnp.concatenate([edge[h, 0, NX + i_low], edge[h, 1, NX + i_up]], axis=0)
            s_main = dot_nt(k_main, q)
            s_tab = dot_nt(k_tab, q)
            s_edge = dot_nt(k_edge, q)
            block = 2 * (xq * ring + pos)
            pieces = []
            for xs in range(NX):
                slot = (xs + NX - xq - 1) % NX
                row = jnp.minimum(slot, SLOTS - 1)
                first = rand_ref[row, x * hx + h, block] % 2
                second = rand_ref[row, x * hx + h, block + 1] % 2
                own = jnp.where(slot == SLOTS, 1, 0)
                inside = jnp.where(half == 0, first, second)
                for b in range(2):
                    hit = jnp.where(inside == b, 1, own)
                    keep = jnp.broadcast_to(hit, (BLK, 2 * BLK)) > 0
                    at = (xs * 2 + b) * BLK
                    pieces.append(jnp.where(keep, s_main[at : at + BLK], -1e30))
            pieces += [s_tab[:BLK], s_tab[BLK:]]
            ok_low = jnp.where(jnp.logical_and(xq == 0, pos == 0), 0, 1)
            ok_up = jnp.where(jnp.logical_and(xq == NX - 1, pos == ring - 1), 0, 1)
            for b, ok in ((0, ok_low), (1, ok_up)):
                hit = jnp.where(half == b, ok, 0)
                keep = jnp.broadcast_to(hit, (BLK, 2 * BLK)) > 0
                pieces.append(jnp.where(keep, s_edge[b * BLK : (b + 1) * BLK], -1e30))
            top = functools.reduce(jnp.maximum, pieces)
            top = jnp.max(top, axis=0, keepdims=True)
            exps = [jnp.exp2((piece - top) * (scaling * math.log2(math.e))) for piece in pieces]
            total = jnp.sum(functools.reduce(jnp.add, exps), axis=0, keepdims=True)
            inverse = 1.0 / total
            d_main = dot_nt(v_main, g)
            d_tab = dot_nt(v_tab, g)
            d_edge = dot_nt(v_edge, g)
            d_pieces = [d_main[i * BLK : (i + 1) * BLK] for i in range(2 * NX)]
            d_pieces += [d_tab[:BLK], d_tab[BLK:], d_edge[:BLK], d_edge[BLK:]]
            probs = [e * inverse for e in exps]
            probs_b = [p.astype(BF16) for p in probs]
            dots = functools.reduce(
                jnp.add, [p.astype(F32) * d for p, d in zip(probs_b, d_pieces)]
            )
            row_dot = jnp.sum(dots, axis=0, keepdims=True)
            grads = [
                (p * (d - row_dot) * scaling).astype(BF16) for p, d in zip(probs, d_pieces)
            ]
            cols = pl.ds(pl.multiple_of(xq * 2 * BLK, 2 * BLK), 2 * BLK)
            pt[:, cols] = jnp.concatenate(probs_b, axis=0)
            dst[:, cols] = jnp.concatenate(grads, axis=0)
            return carry

        for t in range(2, 4):
            local_in[h, t].wait()
        lax.fori_loop(0, NX, span, 0)

    last_row = NX * 2 * BLK
    tab_row = last_row + 2 * BLK

    def tables(h):
        for t, lists in ((0, dst), (1, pt)):
            rows = qd[h, t * NX : (t + 1) * NX].reshape(NX * 2 * BLK, HS)
            grad = dot_nn(lists[last_row:tab_row], rows).reshape(2, BLK, HS)
            gp[h, t] = grad
            gpb[h, t] = grad.astype(BF16)
        copy = remote(gpb.at[h, 1 - c], g_core.at[h], c_snd.at[h], c_rcv.at[h], sib, y)
        copy.start()
        core_copies[h] = copy
        sends.append(copy)

    def edges_of(h, t, xs):
        i_low = (xs + NX - seam_low) % NX + t * NX
        i_up = (xs + seam_up) % NX + t * NX
        return jnp.concatenate([edge[h, 0, i_low], edge[h, 1, i_up]], axis=0), i_low, i_up

    def mains(h):
        dq = dot_tn(dst[:last_row], kv[h, 0:NX].reshape(last_row, HS))
        dq += dot_tn(dst[last_row:tab_row], gsel[h, 0].reshape(2 * BLK, HS))
        for xs in range(NX):
            part = slice(xs * 2 * BLK, (xs + 1) * 2 * BLK)
            k_edge = edges_of(h, 0, xs)[0]
            dq_edge = dot_tn(dst[tab_row:, part], k_edge)
            dqs[h, xs] = (dq[part] + dq_edge).astype(BF16).reshape(2, BLK, HS)
            for t, lists in ((0, dst), (1, pt)):
                rows = qd[h, t * NX + xs].reshape(2 * BLK, HS)
                grad = dot_nn(lists[tab_row:, part], rows).astype(BF16)
                _, i_low, i_up = edges_of(h, t, xs)
                edge_s[h, 0, i_low] = grad[:BLK]
                edge_s[h, 1, i_up] = grad[BLK:]
        for t, lists in ((0, dst), (1, pt)):
            rows = qd[h, t * NX : (t + 1) * NX].reshape(NX * 2 * BLK, HS)
            grad = dot_nn(lists[:last_row], rows)
            dkv[h, t * NX : (t + 1) * NX] = grad.reshape(NX, 2, BLK, HS)

    core_copies = {}
    back_copies = {}
    pending = []
    locals_out = []

    def out_cols(xs, h):
        return pl.ds(pl.multiple_of(xs * wide + h * HS, HS), HS)

    def send_out(out, src_of, h, snd, rcv, loc):
        for j in (2, 1, 3):
            to = at_x(j)
            copy = remote(
                src_of(to), out.at[:, :, out_cols(x, h)], snd(j - 1), rcv(j - 1), ctx_x(to), y
            )
            copy.start()
            sends.append(copy)
            frm = at_x(NX - j)
            pending.append(
                remote(
                    src_of(to), out.at[:, :, out_cols(frm, h)], snd(j - 1), rcv(j - 1), ctx_x(to), y
                )
            )
        copy = pltpu.make_async_copy(src_of(x), out.at[:, :, out_cols(x, h)], loc)
        copy.start()
        locals_out.append(copy)

    def send_back(h):
        for way, to in ((0, low), (1, up)):
            copy = remote(
                edge_s.at[h, way], edge_r.at[h, way], b_snd.at[h, way], b_rcv.at[h, way], to, y
            )
            copy.start()
            back_copies[h, way] = copy
            sends.append(copy)

    def send_dq(h):
        send_out(
            dq_out,
            lambda xs: dqs.at[h, xs],
            h,
            lambda j: dq_snd.at[h, j],
            lambda j: dq_rcv.at[h, j],
            dq_loc.at[h],
        )

    def finish(h):
        for way in range(2):
            back_copies[h, way].wait_recv()
        for t in range(2):
            for b in range(2):
                part = slice(t * NX, (t + 1) * NX)
                total = dkv[h, part, b] + edge_r[h, 1 - b, part].astype(F32)
                dkvb[h, part, b] = total.astype(BF16)
        for t, out in ((0, dk_out), (1, dv_out)):
            send_out(
                out,
                lambda xs, t=t: dkvb.at[h, t * NX + xs],
                h,
                lambda j, t=t: dkv_snd.at[h, t, j],
                lambda j, t=t: dkv_rcv.at[h, t, j],
                dkv_loc.at[h, t],
            )

    rows_y = BLK // ny

    def y_start(h):
        core_copies[h].wait_recv()
        for s in range(2):
            both = (gp[h, c, s] + g_core[h, s].astype(F32)).astype(BF16)
            for r in range(ny):
                y_send[h, r, s] = both[r * rows_y : (r + 1) * rows_y]
        for j in outward(ny):
            to = (y + j) % ny
            copy = remote(
                y_send.at[h, to], y_recv.at[h, y], yr_snd.at[h, j - 1], yr_rcv.at[h, j - 1], ctx, to
            )
            copy.start()
            sends.append(copy)
        y_recv[h, y] = y_send[h, y]

    def z_start(h):
        for j in outward(ny)[::-1]:
            frm = (y + ny - j) % ny
            remote(
                y_send.at[h, y], y_recv.at[h, frm], yr_snd.at[h, j - 1], yr_rcv.at[h, j - 1], ctx, frm
            ).wait_recv()
        sums = [jnp.zeros((rows_y, HS), F32) for _ in range(TABLE)]
        for src in range(ny):
            for s in range(2):
                chosen = ids_all[src, s]
                term = y_recv[h, src, s].astype(F32)
                sums = [acc + jnp.where(chosen == b, term, 0.0) for b, acc in enumerate(sums)]
        for b in range(TABLE):
            z_all[h, z, b] = sums[b].astype(BF16)
        for j in outward(nz):
            to = (z + j) % nz
            copy = remote(
                z_all.at[h, z], z_all.at[h, z], z_snd.at[h, j - 1], z_rcv.at[h, j - 1], ctx_z(to), y
            )
            copy.start()
            sends.append(copy)

    def z_end(h):
        for j in outward(nz)[::-1]:
            frm = (z + nz - j) % nz
            remote(
                z_all.at[h, frm], z_all.at[h, frm], z_snd.at[h, j - 1], z_rcv.at[h, j - 1], ctx_z(frm), y
            ).wait_recv()
        total = z_all[h, 0].astype(F32)
        for k in range(1, nz):
            total += z_all[h, k].astype(F32)
        y_all[y, h] = total.astype(BF16)

    id_waits = []

    def send_ids():
        for j in range(1, ny):
            to, frm = (y + j) % ny, (y + ny - j) % ny
            copy = remote(ids_all.at[y], ids_all.at[y], id_snd.at[j - 1], id_rcv.at[j - 1], ctx, to)
            copy.start()
            sends.append(copy)
            id_waits.append(
                remote(ids_all.at[frm], ids_all.at[frm], id_snd.at[j - 1], id_rcv.at[j - 1], ctx, frm)
            )

    last = hx - 1
    for h in range(hx):
        send_edges(h)
    hear_word(1)
    for h in range(hx):
        for way in range(2):
            edge_copies[h, way].wait_recv()
        if h == 0:
            hear_word(2)
        compute(h)
        if h == 0:
            hear_word(3)
            send_ids()
        tables(h)
        if h < last:
            mains(h)
            send_back(h)
            hear_word(4)
            y_start(h)
    hear_word(5)
    for copy in id_waits:
        copy.wait_recv()
    for h in range(last):
        z_start(h)
    y_start(last)
    mains(last)
    send_back(last)
    for h in range(hx):
        send_dq(h)
    for h in range(last):
        finish(h)
    z_start(last)
    finish(last)
    for h in range(hx):
        z_end(h)

    def table_out(kind, yy, xs):
        return dg_out.at[kind, xs, yy]

    for j in outward(ny)[::-1]:
        to = (y + j) % ny
        copy = remote(y_all.at[y], y_all.at[y], yg_snd.at[j - 1], yg_rcv.at[j - 1], ctx, to)
        copy.start()
        sends.append(copy)

    def to_sibling(src, yy, xs, j, d):
        copy = remote(src, table_out(c, yy, xs), cg_snd.at[j, d], cg_rcv.at[j, d], sib, y)
        copy.start()
        sends.append(copy)
        pending.append(
            remote(src, table_out(1 - c, yy, xs), cg_snd.at[j, d], cg_rcv.at[j, d], sib, y)
        )

    def spread(d):
        yy = (y + ny - d) % ny
        for j in (2, 1, 3):
            copy = remote(
                y_all.at[yy],
                table_out(c, yy, x),
                xg_snd.at[j - 1, d],
                xg_rcv.at[j - 1, d],
                ctx_x(at_x(j)),
                y,
            )
            copy.start()
            sends.append(copy)
        to_sibling(y_all.at[yy], yy, x, 0, d)
        copy = pltpu.make_async_copy(y_all.at[yy], table_out(c, yy, x), xg_loc.at[d])
        copy.start()
        locals_out.append(copy)

    def pass_on(d):
        yy = (y + ny - d) % ny
        for j in (1, 3, 2):
            frm = at_x(NX - j)
            remote(
                y_all.at[yy],
                table_out(c, yy, frm),
                xg_snd.at[j - 1, d],
                xg_rcv.at[j - 1, d],
                ctx_x(frm),
                y,
            ).wait_recv()
            to_sibling(table_out(c, yy, frm), yy, frm, j, d)

    near = outward(ny)[::-1]
    spread(0)
    for d in near:
        frm = (y + ny - d) % ny
        remote(y_all.at[frm], y_all.at[frm], yg_snd.at[d - 1], yg_rcv.at[d - 1], ctx, frm).wait_recv()
        spread(d)
    for d in [0] + near:
        pass_on(d)

    for copy in locals_out:
        copy.wait()
    for copy in pending:
        copy.wait_recv()
    for copy in sends:
        copy.wait_send()


def last_step(dq_in, dk_in, dv_in, dg_in, dq_out, dk_out, dv_out, dg_out, full, put):
    kinds, parts, _, heads = dg_in.shape[:4]
    stores = []
    for kind in range(kinds):
        for xs in range(parts):
            i = kind * parts + xs
            for h in range(heads):
                for b in range(TABLE):
                    rows_b = dg_in[kind, xs, :, h, b].astype(F32).reshape(BLK, HS)
                    full[i, b, :, h * HS : (h + 1) * HS] = rows_b
            cols = pl.ds(xs * full.shape[3], full.shape[3])
            stores.append(
                pltpu.make_async_copy(full.at[i], dg_out.at[kind, :, :, cols], put.at[i])
            )
            stores[-1].start()
    for i, (src, dst_ref) in enumerate(((dq_in, dq_out), (dk_in, dk_out), (dv_in, dv_out))):
        stores.append(pltpu.make_async_copy(src, dst_ref, put.at[kinds * parts + i]))
        stores[-1].start()
    for copy in stores:
        copy.wait()


def on_device(nz, ny, query, key, value, dout, glob_keys, glob_values, glob_ids, rand_blocks):
    heads = rand_blocks.shape[0]
    hx = heads // NX
    hd = query.shape[2]
    wide = hx * HS
    rows_y = BLK // ny
    blocks = [a.reshape(2, BLK, hd) for a in (query, key, value, dout)]
    rand = jnp.transpose(rand_blocks, (2, 0, 1))
    operands = (glob_ids, rand, *blocks, glob_keys, glob_values)
    vm = pltpu.VMEM
    dma = pltpu.SemaphoreType.DMA
    out = jax.ShapeDtypeStruct((2, BLK, hd), BF16)
    anywhere = pl.BlockSpec(memory_space=pltpu.HBM)
    scratch = [
        vm((hx, 2 * NX, 2, BLK, HS), BF16),
        vm((hx, 2 * NX, 2, BLK, HS), BF16),
        vm((hx, 2, 2 * NX, BLK, HS), BF16),
        vm((2, TABLE, BLK, wide), BF16),
        vm((hx, 2, 2, BLK, HS), BF16),
        vm((12 * BLK, NX * 2 * BLK), BF16),
        vm((12 * BLK, NX * 2 * BLK), BF16),
        vm((hx, NX, 2, BLK, HS), BF16),
        vm((hx, 2 * NX, 2, BLK, HS), F32),
        vm((hx, 2 * NX, 2, BLK, HS), BF16),
        vm((hx, 2, 2 * NX, BLK, HS), BF16),
        vm((hx, 2, 2 * NX, BLK, HS), BF16),
        vm((hx, 2, 2, BLK, HS), F32),
        vm((hx, 2, 2, BLK, HS), BF16),
        vm((hx, 2, BLK, HS), BF16),
        vm((ny, 2, rows_y, HS), jnp.int32),
        vm((hx, ny, 2, rows_y, HS), BF16),
        vm((hx, ny, 2, rows_y, HS), BF16),
        vm((hx, nz, TABLE, rows_y, HS), BF16),
        vm((ny, hx, TABLE, rows_y, HS), BF16),
        dma((hx, 4)),
        dma((hx, 4, 3)),
        dma((hx, 4, 3)),
        dma((2,)),
        dma((hx, 2)),
        dma((hx, 2)),
        dma((hx, 2)),
        dma((hx, 2)),
        dma((hx,)),
        dma((hx, 3)),
        dma((hx, 3)),
        dma((hx, 2)),
        dma((hx, 2, 3)),
        dma((hx, 2, 3)),
        dma((hx,)),
        dma((hx,)),
        dma((ny,)),
        dma((ny,)),
        dma((hx, ny)),
        dma((hx, ny)),
        dma((hx, nz)),
        dma((hx, nz)),
        dma((ny,)),
        dma((ny,)),
        dma((ny,)),
        dma((3, ny)),
        dma((3, ny)),
        dma((4, ny)),
        dma((4, ny)),
        pltpu.SemaphoreType.REGULAR((max(ny, nz) // 2, 4)),
        pltpu.SMEM(glob_ids.shape, jnp.int32),
        pltpu.SMEM(rand.shape, jnp.int32),
        dma((2,)),
    ]
    dq, dk, dv, dg = pl.pallas_call(
        functools.partial(body, nz, ny, hx),
        out_shape=(out, out, out, jax.ShapeDtypeStruct((2, NX, ny, hx, TABLE, rows_y, HS), BF16)),
        in_specs=[pl.BlockSpec(memory_space=pltpu.HBM)] * 8,
        out_specs=(anywhere,) * 4,
        scratch_shapes=scratch,
        compiler_params=pltpu.CompilerParams(
            collective_id=0, has_side_effects=True, vmem_limit_bytes=40 * 1024 * 1024
        ),
    )(*[pltpu.with_memory_space_constraint(a, pltpu.HBM) for a in operands])
    rows = jax.ShapeDtypeStruct((1, 2 * BLK, hd), BF16)
    dq, dk, dv = (a.reshape(1, 2 * BLK, hd) for a in (dq, dk, dv))
    parts = 2 * NX
    return tuple(
        pl.pallas_call(
            last_step,
            out_shape=(rows, rows, rows, jax.ShapeDtypeStruct((2, TABLE, BLK, hd), F32)),
            in_specs=[pl.BlockSpec(memory_space=pltpu.VMEM)] * 4,
            out_specs=(anywhere,) * 4,
            scratch_shapes=[
                vm((parts, TABLE, BLK, wide), F32),
                dma((parts + 3,)),
            ],
            compiler_params=pltpu.CompilerParams(vmem_limit_bytes=16 * 1024 * 1024),
        )(dq, dk, dv, dg)
    )


def solution(mesh):
    ny = mesh.shape["dp"]
    nz = mesh.shape["ctx"] // (2 * NX)
    split = P("dp", "ctx", None)
    return jax.shard_map(
        functools.partial(on_device, nz, ny),
        mesh=mesh,
        in_specs=(split, split, split, split, P(), P(), P("dp", None), P()),
        out_specs=(split, split, split, P()),
        check_vma=False,
    )
```
